32 devices in a mesh: ctx: 4 (over y, x), fsdp: 8 (over z, core).
Axes of the slice: x: 2, y: 2, z: 4, core: 2. Of those that a mesh axis runs over, the one named last changes fastest.
Arguments:
- tokens: bfloat16 [8, 512, 2048], P('fsdp', 'ctx'), may hold values from -6 to 6
- cotangent: bfloat16 [8, 512, 2048], P('fsdp', 'ctx'), may hold values from -6 to 6
- block_ids: int32 [8, 512], P('fsdp', 'ctx'), may hold values from 0 to 2, as said below
- span_order: int32 [8, 8], P('fsdp'), may hold values from 0 to 7, as said below
- attn_gain: bfloat16 [2048], P('fsdp'), may hold values from 0.099609375 to 1.8984375
- w_qkv: bfloat16 [2048, 3, 2048], P('fsdp'), may hold values from -0.125 to 0.125
- w_out: bfloat16 [2048, 2048], P('fsdp'), may hold values from -0.75 to 0.75
- ffn_gain: bfloat16 [2048], P('fsdp'), may hold values from 0.099609375 to 1.8984375
- w_gate_up: bfloat16 [2048, 2, 8192], P('fsdp'), may hold values from -0.125 to 0.125
- w_down: bfloat16 [8192, 2048], P('fsdp'), may hold values from -0.0625 to 0.0625
Outputs:
- layer_out: bfloat16 [8, 512, 2048], P('fsdp', 'ctx')
- input_grad: bfloat16 [8, 512, 2048], P('fsdp', 'ctx')
- grad_attn_gain: float32 [2048], P('fsdp')
- grad_qkv: float32 [2048, 3, 2048], P('fsdp')
- grad_out: float32 [2048, 2048], P('fsdp')
- grad_ffn_gain: float32 [2048], P('fsdp')
- grad_gate_up: float32 [2048, 2, 8192], P('fsdp')
- grad_down: float32 [8192, 2048], P('fsdp')
The draws below stay inside these ranges and needn't reach their ends.
Inputs may be any that keep to these rules, and one draw needn't show every extreme that they name: Each row is an ordering of 0 to 7; stored row i of a sequence holds position span_order[s, i // 64] * 64 + i % 64. `block_ids`: in order of positions the block numbers of a sequence start at 0, never fall and rise by one at a time; every sequence has exactly 3 blocks, each covering 1 to 256 consecutive positions, and one block of every sequence covers exactly 256.
All inputs are finite; a program needn't handle non-finite values.
Results may differ from the reference program's by a relative error of at most 0.023.
Values may be sent and summed in bfloat16 or wider, within the bound.
No kernel may reach another device: no remote copies, remote signals or barrier semaphores. Data moves between devices by JAX's collectives and lax.ppermute only.
A program may use at most 576 MiB of HBM per device.

```python
import functools
import math
import jax
import jax.numpy as jnp
from jax import lax

D = 2048
HD = 64
FF = 8192
BLOCK = 256
HALF = 64
SPANS = 8
SEQ_LEN = 512
SEQS = 8


def permute_one(subkey):
    return jax.random.permutation(subkey, SPANS).astype(jnp.int32)


def layout_draw(key):
    order_key = jax.random.fold_in(key, 101)
    length_key = jax.random.fold_in(key, 202)
    choose_key = jax.random.fold_in(key, 303)
    orders = jax.vmap(permute_one)(jax.random.split(order_key, SEQS))
    block_count = 2 * SEQ_LEN // BLOCK - 1
    pair_count = (block_count - 1) // 2
    firsts = jax.random.randint(length_key, (SEQS, pair_count), 1, BLOCK, dtype=jnp.int32)
    pairs = jnp.stack([firsts, BLOCK - firsts], 2).reshape(SEQS, 2 * pair_count)
    full = jnp.concatenate([jnp.full((SEQS, 1), BLOCK, jnp.int32), pairs], 1)
    offset = jax.random.randint(choose_key, (SEQS, 1), 0, block_count, dtype=jnp.int32)
    slots = jnp.arange(block_count, dtype=jnp.int32)
    lengths = jnp.take_along_axis(full, ((slots[None, :] - offset) % block_count).astype(jnp.int32), axis=1)
    finish = jnp.cumsum(lengths, axis=1).astype(jnp.int32)
    places = jnp.arange(SEQ_LEN, dtype=jnp.int32)
    search = functools.partial(jnp.searchsorted, side='right')
    natural = jax.vmap(search, in_axes=(0, None))(finish, places).astype(jnp.int32)
    span_index = jnp.broadcast_to((places // HALF)[None, :], (SEQS, SEQ_LEN))
    positions = jnp.take_along_axis(orders, span_index, axis=1) * HALF + places[None, :] % HALF
    blocks = jnp.take_along_axis(natural, positions.astype(jnp.int32), axis=1)
    return (orders, blocks.astype(jnp.int32))


def draw_span_order(key, part):
    return layout_draw(key)[0]


def draw_block_ids(key, part):
    return layout_draw(key)[1]


def steps_of(stream_key, shape, cuts, low, top_value):
    level = 1.0
    for dim, shards_of in cuts:
        draws = jax.random.uniform(jax.random.fold_in(jax.random.fold_in(stream_key, 6), dim), (shards_of,), jnp.float32, low / len(cuts), top_value / len(cuts))
        level = level * jnp.repeat(jnp.exp(draws), shape[dim] // shards_of).reshape((-1,) + (1,) * (len(shape) - 1 - dim))
    return level


def normal_values(own_key, dims, scale, most, cuts=(), kind=jnp.bfloat16):
    array = scale * jax.random.normal(own_key, dims, jnp.float32)
    if cuts:
        array = array * steps_of(own_key, dims, cuts, -0.22, 0.18)
    return jnp.clip(array, -most, most).astype(kind)


def setup_inputs(seed: int = 0) -> dict:
    splits = jax.random.split(jax.random.key(seed), 11)
    tokens = normal_values(splits[0], (SEQS, SEQ_LEN, D), 1.0, 6.0, ((0, 8), (1, 4)))
    cotangent = normal_values(splits[1], (SEQS, SEQ_LEN, D), 1.0, 6.0, ((0, 8), (1, 4)))
    block_ids = draw_block_ids(jax.random.fold_in(splits[10], 71), 0)
    span_order = draw_span_order(jax.random.fold_in(splits[10], 71), 0)
    attn_gain = jnp.clip(1.0 + 0.18 * jax.random.normal(splits[4], (D,), jnp.float32), 0.099609375, 1.8984375).astype(jnp.bfloat16)
    w_qkv = normal_values(splits[5], (D, 3, D), D ** -0.5, 0.125, ((0, 8),))
    w_out = normal_values(splits[6], (D, D), (max(16 * D // SEQ_LEN, 1)) ** -0.5, 0.75, ((0, 8),))
    ffn_gain = jnp.clip(1.0 + 0.18 * jax.random.normal(splits[7], (D,), jnp.float32), 0.099609375, 1.8984375).astype(jnp.bfloat16)
    w_gate_up = normal_values(splits[8], (D, 2, FF), D ** -0.5, 0.125, ((0, 8),))
    w_down = normal_values(splits[9], (FF, D), FF ** -0.5, 0.0625, ((0, 8),))
    return {"tokens": tokens, "cotangent": cotangent, "block_ids": block_ids, "span_order": span_order, "attn_gain": attn_gain, "w_qkv": w_qkv, "w_out": w_out, "ffn_gain": ffn_gain, "w_gate_up": w_gate_up, "w_down": w_down}


@jax.custom_vjp
def low(v):
    return lax.optimization_barrier(v.astype(jnp.bfloat16)).astype(jnp.float32)

@jax.custom_vjp
def low_back(v):
    return v

def low_keep(v):
    return (low(v), None)

def low_pass(kept, grad):
    return (grad,)

def back_keep(v):
    return (v, None)

def back_low(kept, grad):
    return (low(grad),)
low.defvjp(low_keep, low_pass)
low_back.defvjp(back_keep, back_low)
rope_theta = 130000.0
norm_eps = 1e-05
score_scale = 0.125
masked_score = -1e+30
highest = lax.Precision.HIGHEST

def angles(positions, width):
    half_width = width // 2
    frequency = rope_theta ** (-2.0 * jnp.arange(half_width, dtype=jnp.float32) / width)
    phases = positions.astype(jnp.float32)[:, None] * frequency[None, :]
    return (jnp.cos(phases)[:, None, :], jnp.sin(phases)[:, None, :])

def rotate(values, cosine, sine):
    half_width = values.shape[-1] // 2
    leading = values[..., :half_width]
    trailing = values[..., half_width:]
    return jnp.concatenate([leading * cosine - trailing * sine, trailing * cosine + leading * sine], -1)

def rms_norm(values):
    return values * lax.rsqrt(lax.optimization_barrier(jnp.mean(values * values, -1, keepdims=True)) + norm_eps)

def attend(query, keys_all, values_all, blocks):
    length = query.shape[0]
    rows_step = math.gcd(length, 512)
    count = length // rows_step

    def one_block(item):
        query_part, block_part = item
        scores = low_back(jnp.einsum('qhe,khe->qhk', query_part, keys_all, precision=highest) * score_scale)
        allowed = blocks[None, None, :] <= block_part[:, None, None]
        scores = jnp.where(allowed, scores, masked_score)
        peak = lax.optimization_barrier(jnp.max(scores, -1, keepdims=True))
        log_total = peak + jnp.log(lax.optimization_barrier(jnp.sum(jnp.exp(scores - peak), -1, keepdims=True)))
        probs = low(jnp.exp(scores - log_total))
        return jnp.einsum('qhk,khe->qhe', probs, values_all, precision=highest)
    result = lax.map(jax.checkpoint(one_block), (query.reshape(count, rows_step, query.shape[1], query.shape[2]), blocks.reshape(count, rows_step)))
    return result.reshape(query.shape)

def layer(params, inputs, positions, blocks):
    attn_gain, qkv_weight, out_weight, ffn_gain, gate_up_weight, down_weight = params
    length, width = inputs.shape
    heads = width // HD
    cosine, sine = angles(positions, HD)
    act_one = low(rms_norm(inputs) * attn_gain)
    qkv = low_back(jnp.einsum('td,dke->tke', act_one, qkv_weight, precision=highest))
    query = low(rotate(qkv[:, 0].reshape(length, heads, HD), cosine, sine))
    keys_all = low(rotate(qkv[:, 1].reshape(length, heads, HD), cosine, sine))
    values_all = low(qkv[:, 2].reshape(length, heads, HD))
    attended = attend(query, keys_all, values_all, blocks)
    attn_b = low(low_back(attended.reshape(length, width)))
    resid = inputs + low_back(jnp.dot(attn_b, out_weight, precision=highest))
    act_two = low(rms_norm(resid) * ffn_gain)
    gate_up = low_back(jnp.einsum('td,dkf->tkf', act_two, gate_up_weight, precision=highest))
    hidden = low(jax.nn.silu(gate_up[:, 0]) * gate_up[:, 1])
    return resid + jnp.dot(hidden, down_weight, precision=highest)

def reference(tokens, cotangent, block_ids, span_order, attn_gain, w_qkv, w_out, ffn_gain, w_gate_up, w_down):
    params = tuple((weight.astype(jnp.float32) for weight in (attn_gain, w_qkv, w_out, ffn_gain, w_gate_up, w_down)))
    row_ids = jnp.arange(SEQ_LEN, dtype=jnp.int32)

    def one_sequence(totals, item):
        seq_tokens, seq_cot, seq_blocks, seq_order = item
        positions = seq_order[row_ids // HALF] * HALF + row_ids % HALF
        forward = functools.partial(layer, positions=positions, blocks=seq_blocks)
        output, pullback = jax.vjp(forward, params, seq_tokens.astype(jnp.float32))
        grad_params, grad_inputs = pullback(seq_cot.astype(jnp.float32))
        totals = jax.tree.map(jnp.add, totals, grad_params)
        return (totals, (output.astype(jnp.bfloat16), grad_inputs.astype(jnp.bfloat16)))
    initial = jax.tree.map(jnp.zeros_like, params)
    totals, stacked = lax.scan(one_sequence, initial, (tokens, cotangent, block_ids, span_order))
    return (stacked[0], stacked[1], totals[0], totals[1], totals[2], totals[3], totals[4], totals[5])
```

```python
import jax
import jax.numpy as jnp
from jax import lax
from jax.sharding import PartitionSpec as P

HD = 64

rope_theta = 130000.0
norm_eps = 1e-05
score_scale = 0.125
masked_score = -1e30


def swapped(array, axis, by):
    size = lax.axis_size(axis)
    return lax.ppermute(array, axis, [(i, i ^ by) for i in range(size)])


def gathered(array, axis):
    return [array] + [swapped(array, axis, k) for k in range(1, lax.axis_size(axis))]


def scattered(parts, axis):
    total = parts[0].astype(jnp.float32)
    for k in range(1, lax.axis_size(axis)):
        total = total + swapped(parts[k].astype(jnp.bfloat16), axis, k).astype(jnp.float32)
    return total


def exchanged(blocks, axis):
    size = lax.axis_size(axis)
    own = lax.axis_index(axis)
    result = blocks
    for k in range(1, size):
        other = own ^ k
        block = lax.dynamic_index_in_dim(blocks, other, 0, keepdims=True)
        result = lax.dynamic_update_slice_in_dim(result, swapped(block, axis, k), other, 0)
    return result


def angles(positions, width):
    half_width = width // 2
    frequency = rope_theta ** (-2.0 * jnp.arange(half_width, dtype=jnp.float32) / width)
    phases = positions.astype(jnp.float32)[:, None] * frequency[None, :]
    return (jnp.cos(phases)[:, None, :], jnp.sin(phases)[:, None, :])


def rotate(values, cosine, sine):
    half_width = values.shape[-1] // 2
    leading = values[..., :half_width]
    trailing = values[..., half_width:]
    return jnp.concatenate(
        [leading * cosine - trailing * sine, trailing * cosine + leading * sine], -1
    )


def inverse_rms(values):
    return lax.rsqrt(jnp.mean(values * values, -1, keepdims=True) + norm_eps)


def norm_back(grad_normed, normed, gain, inverse):
    scaled = grad_normed * gain
    return inverse * (scaled - normed * jnp.mean(scaled * normed, -1, keepdims=True))


def product(left, right, left_dim, right_dim):
    return lax.dot_general(
        left, right, (((left_dim,), (right_dim,)), ((), ())), preferred_element_type=jnp.float32
    )


def low(values):
    return values.astype(jnp.bfloat16)


def gather_rows(array, axis):
    return lax.all_gather(array, axis, axis=0, tiled=True)


def scatter_rows(array, axis):
    return lax.psum_scatter(low(array), axis, scatter_dimension=0, tiled=True)


def per_device(
    tokens, cotangent, block_ids, span_order, attn_gain, w_qkv, w_out, ffn_gain, w_gate_up, w_down
):
    ctx_count = lax.axis_size("ctx")
    fsdp_count = lax.axis_size("fsdp")
    ctx = lax.axis_index("ctx")
    rows = tokens.shape[1]
    width = tokens.shape[2]
    shard = w_qkv.shape[0]
    length = rows * ctx_count
    heads = width // HD // ctx_count
    own_width = heads * HD
    inputs = tokens[0].astype(jnp.float32)
    strided = (shard // HD) % ctx_count == 0

    chunks = jnp.bitwise_xor(ctx, jnp.arange(ctx_count, dtype=jnp.int32))
    order_row = span_order[0]
    spans = order_row.shape[0]
    half = length // spans
    local = jnp.arange(rows, dtype=jnp.int32)
    slots = (chunks[:, None] * (rows // half) + (local // half)[None, :]).reshape(length)
    matches = slots[:, None] == jnp.arange(spans, dtype=jnp.int32)[None, :]
    picked = jnp.sum(jnp.where(matches, order_row[None, :], 0), axis=1)
    positions = picked * half + jnp.tile(local % half, ctx_count)
    cosine, sine = angles(positions, HD)
    blocks = jnp.concatenate(gathered(block_ids[0], "ctx"), 0)
    allowed = (blocks[None, :] <= blocks[:, None])[None]

    if strided:
        per = heads // fsdp_count
        qkv_own = lax.dynamic_index_in_dim(
            w_qkv.reshape(shard, 3, fsdp_count, ctx_count, per * HD), ctx, 3, keepdims=False
        ).reshape(shard, 3 * own_width)
        out_own = lax.dynamic_slice_in_dim(w_out, ctx * (per * HD), per * HD, 0)
        qkv_weight = gather_rows(qkv_own, "fsdp")
        out_weight = gather_rows(out_own, "fsdp")
    else:
        qkv_own = lax.dynamic_slice_in_dim(w_qkv, ctx * own_width, own_width, 2)
        qkv_weight = gather_rows(qkv_own.reshape(shard, 3 * own_width), "fsdp")
        out_weight = lax.dynamic_slice_in_dim(
            gather_rows(w_out, "fsdp"), ctx * own_width, own_width, 0
        )
    gains = lax.all_gather(
        jnp.stack([attn_gain, ffn_gain]), "fsdp", axis=1, tiled=True
    ).astype(jnp.float32)
    gain_one, gain_two = gains[0], gains[1]

    hidden_own = w_down.shape[0]
    block = hidden_own // ctx_count
    gate_up_own = lax.dynamic_index_in_dim(
        w_gate_up.reshape(shard, 2, fsdp_count, ctx_count, block), ctx, 3, keepdims=False
    )
    gate_up_mine = exchanged(jnp.transpose(gate_up_own, (2, 0, 1, 3)), "fsdp")
    gate_up_mine = gate_up_mine.reshape(width, 2, block)
    gate_up_weight = jnp.stack(gathered(gate_up_mine, "ctx"), 2).reshape(width, 2 * hidden_own)
    down_weight = jnp.concatenate(
        [
            lax.dynamic_slice_in_dim(w_down, (ctx ^ k) * block, block, 0)
            for k in range(ctx_count)
        ],
        0,
    )

    inverse_one = inverse_rms(inputs)
    normed_one = inputs * inverse_one
    act_one = low(normed_one * gain_one)
    act_seq = jnp.concatenate(gathered(act_one, "ctx"), 0)
    qkv = product(act_seq, qkv_weight, 1, 0).reshape(length, 3, heads, HD)
    query = low(rotate(qkv[:, 0], cosine, sine))
    keys = low(rotate(qkv[:, 1], cosine, sine))
    values = low(qkv[:, 2])
    scores = (
        jnp.einsum("qhe,khe->hqk", query, keys, preferred_element_type=jnp.float32) * score_scale
    )
    scores = jnp.where(allowed, scores, masked_score)
    top = jnp.max(scores, -1, keepdims=True)
    weights = jnp.where(allowed, jnp.exp(scores - top), 0.0)
    total = jnp.sum(weights, -1, keepdims=True)
    probs = weights / total
    probs_b = low(probs)
    attended = jnp.einsum("hqk,khe->qhe", probs_b, values, preferred_element_type=jnp.float32)
    attn_b = low(attended).reshape(length, own_width)
    branch = product(attn_b, out_weight, 1, 0).reshape(ctx_count, rows, width)
    resid = inputs + scattered([branch[k] for k in range(ctx_count)], "ctx")

    inverse_two = inverse_rms(resid)
    normed_two = resid * inverse_two
    act_two = gather_rows(low(normed_two * gain_two), "fsdp")
    cot = gather_rows(cotangent[0], "fsdp")
    gate_up = product(act_two, gate_up_weight, 1, 0)
    gate = gate_up[:, :hidden_own]
    upward = gate_up[:, hidden_own:]
    sigma = jax.nn.sigmoid(gate)
    swish = gate * sigma
    hidden = low(swish * upward)
    layer_out = resid + scatter_rows(product(hidden, down_weight, 1, 0), "fsdp").astype(jnp.float32)
    grad_hidden = product(cot, down_weight, 1, 1)
    grad_gate = grad_hidden * upward * sigma * (1.0 + gate * (1.0 - sigma))
    grad_up = grad_hidden * swish
    grad_gu = low(jnp.concatenate([grad_gate, grad_up], 1))
    grad_act_two = scatter_rows(product(grad_gu, gate_up_weight, 1, 1), "fsdp").astype(jnp.float32)
    grad_gain_two = jnp.sum(grad_act_two * normed_two, 0)
    grad_resid = cotangent[0].astype(jnp.float32) + norm_back(
        grad_act_two, normed_two, gain_two, inverse_two
    )

    grad_branch = jnp.concatenate(gathered(low(grad_resid), "ctx"), 0)
    grad_att = low(product(grad_branch, out_weight, 1, 1)).reshape(length, heads, HD)
    delta = jnp.sum(grad_att.astype(jnp.float32) * attended, -1)
    grad_values = jnp.einsum("hqk,qhe->khe", probs_b, grad_att, preferred_element_type=jnp.float32)
    grad_probs = jnp.einsum("qhe,khe->hqk", grad_att, values, preferred_element_type=jnp.float32)
    grad_scores = low(probs * (grad_probs - delta.T[..., None]))
    grad_query = (
        jnp.einsum("hqk,khe->qhe", grad_scores, keys, preferred_element_type=jnp.float32)
        * score_scale
    )
    grad_keys = (
        jnp.einsum("hqk,qhe->khe", grad_scores, query, preferred_element_type=jnp.float32)
        * score_scale
    )
    grad_qkv = low(
        jnp.stack(
            [rotate(grad_query, cosine, -sine), rotate(grad_keys, cosine, -sine), grad_values], 1
        )
    ).reshape(length, 3 * own_width)
    back = product(grad_qkv, qkv_weight, 1, 1).reshape(ctx_count, rows, width)
    grad_act_one = scattered([back[k] for k in range(ctx_count)], "ctx")
    grad_gain_one = jnp.sum(grad_act_one * normed_one, 0)
    input_grad = low(grad_resid + norm_back(grad_act_one, normed_one, gain_one, inverse_one))

    part_down = product(hidden, cot, 0, 0).reshape(ctx_count, block, width)
    part_down = low(scattered([part_down[k] for k in range(ctx_count)], "ctx"))
    grad_down = gather_rows(part_down, "ctx").astype(jnp.float32)
    part_gu = product(act_two, grad_gu, 0, 0).reshape(width, 2, ctx_count, block)
    part_gu = low(scattered([part_gu[:, :, k] for k in range(ctx_count)], "ctx"))
    part_gu = exchanged(part_gu.reshape(fsdp_count, shard, 2, block), "fsdp")
    part_gu = lax.all_gather(part_gu, "ctx", axis=0)
    grad_gate_up = jnp.transpose(part_gu, (2, 3, 1, 0, 4)).reshape(w_gate_up.shape)
    part_out = product(attn_b, grad_branch, 0, 0)
    if strided:
        part_out = scatter_rows(part_out, "fsdp")
        grad_out = gather_rows(part_out, "ctx").astype(jnp.float32)
    else:
        part_out = gather_rows(low(part_out), "ctx")
        grad_out = scatter_rows(part_out, "fsdp").astype(jnp.float32)
    part_qkv = scatter_rows(product(act_seq, grad_qkv, 0, 0), "fsdp")
    part_qkv = lax.all_gather(part_qkv, "ctx", axis=0)
    if strided:
        part_qkv = part_qkv.reshape(ctx_count, shard, 3, fsdp_count, own_width // fsdp_count)
        part_qkv = jnp.transpose(part_qkv, (1, 2, 3, 0, 4))
    else:
        part_qkv = jnp.transpose(part_qkv.reshape(ctx_count, shard, 3, own_width), (1, 2, 0, 3))
    grad_w_qkv = part_qkv.reshape(w_qkv.shape)
    grad_gains = lax.psum(jnp.stack([grad_gain_one, grad_gain_two]), "ctx")
    grad_gains = lax.psum_scatter(grad_gains, "fsdp", scatter_dimension=1, tiled=True)
    return (
        low(layer_out)[None],
        input_grad[None],
        grad_gains[0],
        grad_w_qkv.astype(jnp.float32),
        grad_out,
        grad_gains[1],
        grad_gate_up.astype(jnp.float32),
        grad_down,
    )


def solution(mesh):
    return jax.shard_map(
        per_device,
        mesh=mesh,
        in_specs=(
            P("fsdp", "ctx", None),
            P("fsdp", "ctx", None),
            P("fsdp", "ctx"),
            P("fsdp", None),
            P("fsdp"),
            P("fsdp", None, None),
            P("fsdp", None),
            P("fsdp"),
            P("fsdp", None, None),
            P("fsdp", None),
        ),
        out_specs=(
            P("fsdp", "ctx", None),
            P("fsdp", "ctx", None),
            P("fsdp"),
            P("fsdp", None, None),
            P("fsdp", None),
            P("fsdp"),
            P("fsdp", None, None),
            P("fsdp", None),
        ),
        check_vma=False,
    )
```

```python
import functools

import jax
import jax.numpy as jnp
from jax import lax
from jax.experimental import pallas as pl
from jax.experimental.pallas import tpu as pltpu
from jax.sharding import PartitionSpec as P

HD = 64

rope_theta = 130000.0
norm_eps = 1e-05
score_scale = 0.125
masked_score = -1e30


def swapped(array, axis, by):
    size = lax.axis_size(axis)
    return lax.ppermute(array, axis, [(i, i ^ by) for i in range(size)])


def gathered(array, axis):
    return [array] + [swapped(array, axis, k) for k in range(1, lax.axis_size(axis))]


def scattered(parts, axis):
    total = parts[0].astype(jnp.float32)
    for k in range(1, lax.axis_size(axis)):
        total = total + swapped(parts[k].astype(jnp.bfloat16), axis, k).astype(jnp.float32)
    return total


def paired(blocks):
    core = lax.axis_index("fsdp") % 2
    grid = blocks.reshape((blocks.shape[0] // 2, 2) + blocks.shape[1:])
    keep = lax.dynamic_index_in_dim(grid, core, 1, keepdims=False)
    got = swapped(lax.dynamic_index_in_dim(grid, 1 - core, 1, keepdims=False), "fsdp", 1)
    return jnp.stack([jnp.where(core == 0, keep, got), jnp.where(core == 0, got, keep)], 1)


def crossing(pairs):
    chip = lax.axis_index("fsdp") // 2
    return [
        lax.dynamic_index_in_dim(pairs, chip ^ k, 0, keepdims=False)
        for k in range(1, pairs.shape[0])
    ]


def crossed(sends):
    return [swapped(send, "fsdp", 2 * k) for k, send in enumerate(sends, 1)]


def in_order(pairs, received):
    chip = lax.axis_index("fsdp") // 2
    for k, pair in enumerate(received, 1):
        pairs = lax.dynamic_update_index_in_dim(pairs, pair, chip ^ k, 0)
    return pairs.reshape((-1,) + pairs.shape[2:])


def first_hop(array):
    size = lax.axis_size("ctx")
    return [array] + [swapped(array, "ctx", k) for k in range(1, 3 if size == 4 else size)]


def second_hop(pieces):
    if lax.axis_size("ctx") != 4:
        return []
    half = pieces[0].shape[0] // 2
    return [swapped(pieces[1][:half], "ctx", 2), swapped(pieces[2][half:], "ctx", 1)]


def first_fold(parts):
    size = lax.axis_size("ctx")
    if size != 4:
        return [swapped(parts[k], "ctx", k) for k in range(1, size)]
    half = parts[0].shape[0] // 2
    return [swapped(parts[3][:half], "ctx", 1), swapped(parts[3][half:], "ctx", 2)]


def folded(parts, halves):
    if lax.axis_size("ctx") != 4:
        return []
    half = parts[0].shape[0] // 2
    over_x = jnp.concatenate([parts[1][:half], plus(parts[1][half:], halves[1])], 0)
    over_y = jnp.concatenate([plus(parts[2][:half], halves[0]), parts[2][half:]], 0)
    return [over_x, over_y]


def second_fold(sends, halves):
    if not sends:
        return halves
    return [swapped(sends[0], "ctx", 1), swapped(sends[1], "ctx", 2)]


def butterfly(array, axis):
    step = 1
    while step < lax.axis_size(axis):
        array = array + swapped(array, axis, step)
        step *= 2
    return array


def plus(*terms):
    return low(sum(term.astype(jnp.float32) for term in terms))


def placed(pieces, shape, block, body, result=None):
    own = lax.axis_index("ctx").astype(jnp.int32)[None]
    for piece, k, index in pieces:

        def out_map(step, own_ref, k=k, index=index):
            return index(own_ref[0] ^ k, step)

        in_specs = [pl.BlockSpec((1,) + piece.shape[1:], lambda step, own_ref: (step, 0, 0))]
        operands = [own, piece]
        aliases = {}
        if result is not None:
            in_specs.append(pl.BlockSpec(memory_space=pl.ANY))
            operands.append(result)
            aliases = {2: 0}
        result = pl.pallas_call(
            body,
            grid_spec=pltpu.PrefetchScalarGridSpec(
                num_scalar_prefetch=1,
                grid=(piece.shape[0],),
                in_specs=in_specs,
                out_specs=pl.BlockSpec(block, out_map),
            ),
            out_shape=jax.ShapeDtypeStruct(shape, jnp.float32),
            input_output_aliases=aliases,
            cost_estimate=pl.CostEstimate(
                flops=piece.size, bytes_accessed=6 * piece.size, transcendentals=0
            ),
        )(*operands)
    return result


def write_pair(own_ref, piece_ref, *refs):
    out_ref = refs[-1]
    half = piece_ref.shape[2] // 2
    out_ref[:, 0, :] = piece_ref[0, :, :half].astype(jnp.float32)
    out_ref[:, 1, :] = piece_ref[0, :, half:].astype(jnp.float32)


def write_rows(own_ref, piece_ref, *refs):
    refs[-1][...] = piece_ref[0].astype(jnp.float32)


def angles(positions, width):
    half_width = width // 2
    frequency = rope_theta ** (-2.0 * jnp.arange(half_width, dtype=jnp.float32) / width)
    phases = positions.astype(jnp.float32)[:, None] * frequency[None, :]
    return (jnp.cos(phases)[:, None, :], jnp.sin(phases)[:, None, :])


def rotate(values, cosine, sine):
    half_width = values.shape[-1] // 2
    leading = values[..., :half_width]
    trailing = values[..., half_width:]
    return jnp.concatenate(
        [leading * cosine - trailing * sine, trailing * cosine + leading * sine], -1
    )


def inverse_rms(values):
    return lax.rsqrt(jnp.mean(values * values, -1, keepdims=True) + norm_eps)


def norm_back(grad_normed, normed, gain, inverse):
    scaled = grad_normed * gain
    return inverse * (scaled - normed * jnp.mean(scaled * normed, -1, keepdims=True))


def product(left, right, left_dim, right_dim):
    return lax.dot_general(
        left, right, (((left_dim,), (right_dim,)), ((), ())), preferred_element_type=jnp.float32
    )


def low(values):
    return values.astype(jnp.bfloat16)


def together(*arrays):
    return lax.optimization_barrier(arrays)


def gather_rows(array, axis):
    return lax.all_gather(array, axis, axis=0, tiled=True)


def scatter_rows(array, axis):
    return lax.psum_scatter(low(array), axis, scatter_dimension=0, tiled=True)


def write_heads(groups, piece_ref, out_ref):
    count = piece_ref.shape[0]
    each = piece_ref.shape[2] // groups
    for group in range(groups):
        row = [
            piece_ref[index, :, group * each : (group + 1) * each].astype(jnp.float32)
            for index in range(count)
        ]
        out_ref[0, :, group * count * each : (group + 1) * count * each] = jnp.concatenate(row, 1)


def own_columns(own_ref, in_ref, out_ref):
    half = in_ref.shape[2]
    out_ref[0, :, :half] = in_ref[:, 0, :]
    out_ref[0, :, half:] = in_ref[:, 1, :]


def per_device(
    tokens, cotangent, block_ids, span_order, attn_gain, w_qkv, w_out, ffn_gain, w_gate_up, w_down
):
    ctx_count = lax.axis_size("ctx")
    fsdp_count = lax.axis_size("fsdp")
    ctx = lax.axis_index("ctx")
    rows = tokens.shape[1]
    width = tokens.shape[2]
    shard = w_qkv.shape[0]
    length = rows * ctx_count
    heads = width // HD // ctx_count
    own_width = heads * HD
    inputs = tokens[0].astype(jnp.float32)
    strided = (shard // HD) % ctx_count == 0

    chunks = jnp.bitwise_xor(ctx, jnp.arange(ctx_count, dtype=jnp.int32))
    order_row = span_order[0]
    spans = order_row.shape[0]
    half = length // spans
    local = jnp.arange(rows, dtype=jnp.int32)
    slots = (chunks[:, None] * (rows // half) + (local // half)[None, :]).reshape(length)
    matches = slots[:, None] == jnp.arange(spans, dtype=jnp.int32)[None, :]
    picked = jnp.sum(jnp.where(matches, order_row[None, :], 0), axis=1)
    positions = picked * half + jnp.tile(local % half, ctx_count)
    cosine, sine = angles(positions, HD)
    blocks = jnp.concatenate(gathered(block_ids[0], "ctx"), 0)
    allowed = (blocks[None, :] <= blocks[:, None])[None]

    if strided:
        per = heads // fsdp_count
        qkv_own = lax.dynamic_index_in_dim(
            w_qkv.reshape(shard, 3, fsdp_count, ctx_count, per * HD), ctx, 3, keepdims=False
        ).reshape(shard, 3 * own_width)
        out_own = lax.dynamic_slice_in_dim(w_out, ctx * (per * HD), per * HD, 0)
        qkv_weight = gather_rows(qkv_own, "fsdp")
        out_weight = gather_rows(out_own, "fsdp")
    else:
        qkv_own = lax.dynamic_slice_in_dim(w_qkv, ctx * own_width, own_width, 2)
        qkv_weight = gather_rows(qkv_own.reshape(shard, 3 * own_width), "fsdp")
        out_weight = lax.dynamic_slice_in_dim(
            gather_rows(w_out, "fsdp"), ctx * own_width, own_width, 0
        )
    gains = lax.all_gather(
        jnp.stack([attn_gain, ffn_gain]), "fsdp", axis=1, tiled=True
    ).astype(jnp.float32)
    gain_one, gain_two = gains[0], gains[1]

    hidden_own = w_down.shape[0]
    part = shard // ctx_count
    gate_up_own = pl.pallas_call(
        own_columns,
        grid_spec=pltpu.PrefetchScalarGridSpec(
            num_scalar_prefetch=1,
            grid=(fsdp_count,),
            in_specs=[pl.BlockSpec((part, 2, hidden_own), lambda step, own: (own[0], 0, step))],
            out_specs=pl.BlockSpec((1, part, 2 * hidden_own), lambda step, own: (step, 0, 0)),
        ),
        out_shape=jax.ShapeDtypeStruct((fsdp_count, part, 2 * hidden_own), jnp.bfloat16),
        cost_estimate=pl.CostEstimate(
            flops=0, bytes_accessed=8 * width * part * fsdp_count, transcendentals=0
        ),
    )(ctx.astype(jnp.int32)[None], w_gate_up)
    inputs, gate_up_own = together(inputs, gate_up_own)
    gate_up_own = paired(gate_up_own)
    gate_up_mine = in_order(gate_up_own, crossed(crossing(gate_up_own)))
    gate_up_mine = gate_up_mine.reshape(fsdp_count * part, 2 * hidden_own)
    gate_up_mine, qkv_weight = together(gate_up_mine, qkv_weight)
    gate_up_pieces = first_hop(gate_up_mine)

    def to_parts(array):
        lead = array.shape[:-1]
        array = array.reshape(lead + (fsdp_count, ctx_count, part))
        array = jnp.swapaxes(array, -3, -2).reshape(lead + (ctx_count, fsdp_count * part))
        return jnp.concatenate(
            [
                lax.dynamic_index_in_dim(array, ctx ^ k, array.ndim - 2, keepdims=False)
                for k in range(ctx_count)
            ],
            -1,
        )

    def from_parts(array):
        lead = array.shape[:-1]
        array = array.reshape(lead + (ctx_count, fsdp_count * part))
        array = jnp.stack(
            [
                lax.dynamic_index_in_dim(array, ctx ^ k, array.ndim - 2, keepdims=False)
                for k in range(ctx_count)
            ],
            -2,
        )
        array = array.reshape(lead + (ctx_count, fsdp_count, part))
        return jnp.swapaxes(array, -3, -2).reshape(lead + (width,))

    inverse_one = inverse_rms(inputs)
    normed_one = inputs * inverse_one
    act_one = low(normed_one * gain_one)
    act_seq = jnp.concatenate(gathered(act_one, "ctx"), 0)
    qkv = product(act_seq, qkv_weight, 1, 0).reshape(length, 3, heads, HD)
    query = low(rotate(qkv[:, 0], cosine, sine))
    keys = low(rotate(qkv[:, 1], cosine, sine))
    values = low(qkv[:, 2])
    scores = (
        jnp.einsum("qhe,khe->hqk", query, keys, preferred_element_type=jnp.float32) * score_scale
    )
    scores = jnp.where(allowed, scores, masked_score)
    top = jnp.max(scores, -1, keepdims=True)
    weights = jnp.where(allowed, jnp.exp(scores - top), 0.0)
    total = jnp.sum(weights, -1, keepdims=True)
    probs = weights / total
    probs_b = low(probs)
    attended = jnp.einsum("hqk,khe->qhe", probs_b, values, preferred_element_type=jnp.float32)
    attn_b = low(attended).reshape(length, own_width)
    branch = product(attn_b, out_weight, 1, 0).reshape(ctx_count, rows, width)
    resid = inputs + scattered([branch[k] for k in range(ctx_count)], "ctx")

    inverse_two = inverse_rms(resid)
    normed_two = resid * inverse_two
    cot = gather_rows(cotangent[0], "fsdp")
    act_two, cot, gate_up_pieces = together(
        to_parts(low(normed_two * gain_two)), cot, gate_up_pieces
    )
    act_two = gather_rows(act_two, "fsdp")
    gate_up_weight = jnp.concatenate(gate_up_pieces + second_hop(gate_up_pieces), 0)
    gate_up = product(act_two, gate_up_weight, 1, 0)
    gate = gate_up[:, :hidden_own]
    upward = gate_up[:, hidden_own:]
    sigma = jax.nn.sigmoid(gate)
    swish = gate * sigma
    hidden = low(swish * upward)
    block = hidden_own // ctx_count
    grad_hidden = product(cot, w_down, 1, 1)
    grad_gate = grad_hidden * upward * sigma * (1.0 + gate * (1.0 - sigma))
    grad_up = grad_hidden * swish
    grad_gu = low(jnp.concatenate([grad_gate, grad_up], 1))
    span = fsdp_count * part

    def gu_term(k):
        return low(product(act_two[:, k * span : (k + 1) * span], grad_gu, 0, 0))

    grad_act_two = low(product(grad_gu, gate_up_weight, 1, 1))
    gu_final = gu_term(ctx_count - 1)
    grad_act_two, grad_gu, gu_final = together(grad_act_two, grad_gu, gu_final)
    grad_act_two = scatter_rows(grad_act_two, "fsdp")
    part_gu = [gu_term(k) for k in range(ctx_count - 1)] + [gu_final]
    gu_halves = first_fold(part_gu)
    out_part = low(product(hidden, w_down, 1, 0))
    part_down = low(product(hidden, cot, 0, 0)).reshape(ctx_count, block, width)
    part_down = [
        lax.dynamic_index_in_dim(part_down, ctx ^ k, 0, keepdims=False) for k in range(ctx_count)
    ]
    part_gu, gu_halves, out_part, part_down = together(part_gu, gu_halves, out_part, part_down)
    gu_sends = folded(part_gu, gu_halves)
    down_halves = first_fold(part_down)
    down_sends = folded(part_down, down_halves)
    grad_act_two, gu_sends, out_part, down_sends = together(
        grad_act_two, gu_sends, out_part, down_sends
    )
    gu_last = second_fold(gu_sends, gu_halves)
    layer_part = scatter_rows(out_part, "fsdp")
    grad_act_two = from_parts(grad_act_two).astype(jnp.float32)
    grad_gain_two = jnp.sum(grad_act_two * normed_two, 0)
    grad_resid = cotangent[0].astype(jnp.float32) + norm_back(
        grad_act_two, normed_two, gain_two, inverse_two
    )

    grad_branch = jnp.concatenate(gathered(low(grad_resid), "ctx"), 0)
    grad_branch, gu_last = together(grad_branch, gu_last)
    gu_pairs = paired(plus(part_gu[0], *gu_last).reshape(fsdp_count, part, 2 * hidden_own))
    grad_att = low(product(grad_branch, out_weight, 1, 1)).reshape(length, heads, HD)
    gu_sends = crossing(gu_pairs)
    part_out = low(product(attn_b, grad_branch, 0, 0))
    grad_att, gu_pairs, gu_sends, down_sends, part_out = together(
        grad_att, gu_pairs, gu_sends, down_sends, part_out
    )
    part_out = scatter_rows(part_out, "fsdp") if strided else part_out
    gu_received = crossed(gu_sends)
    down_last = second_fold(down_sends, down_halves)
    delta = jnp.sum(grad_att.astype(jnp.float32) * attended, -1)
    grad_values = jnp.einsum("hqk,qhe->khe", probs_b, grad_att, preferred_element_type=jnp.float32)
    grad_probs = jnp.einsum("qhe,khe->hqk", grad_att, values, preferred_element_type=jnp.float32)
    grad_scores = low(probs * (grad_probs - delta.T[..., None]))
    grad_query = (
        jnp.einsum("hqk,khe->qhe", grad_scores, keys, preferred_element_type=jnp.float32)
        * score_scale
    )
    grad_keys = (
        jnp.einsum("hqk,qhe->khe", grad_scores, query, preferred_element_type=jnp.float32)
        * score_scale
    )
    grad_qkv = low(
        jnp.stack(
            [rotate(grad_query, cosine, -sine), rotate(grad_keys, cosine, -sine), grad_values], 1
        )
    ).reshape(length, 3 * own_width)
    grad_qkv, down_last, layer_part, gu_received[::2] = together(
        grad_qkv, down_last, layer_part, gu_received[::2]
    )
    down_pieces = first_hop(plus(part_down[0], *down_last))
    part_qkv = low(product(act_seq, grad_qkv, 0, 0))
    back = low(product(grad_qkv, qkv_weight, 1, 1)).reshape(ctx_count, rows, width)
    back = [back[k] for k in range(ctx_count)]
    part_qkv, part_out, back, gu_received, down_pieces = together(
        part_qkv, part_out, back, gu_received, down_pieces
    )
    part_qkv = scatter_rows(part_qkv, "fsdp")

    grad_act_one = scattered(back, "ctx")
    gu_sum = in_order(gu_pairs, gu_received)
    gu_pieces = first_hop(gu_sum)
    grad_act_one, down_pieces = together(grad_act_one, down_pieces)
    down_last = second_hop(down_pieces)
    layer_out = low(resid + layer_part.astype(jnp.float32))
    grad_gain_one = jnp.sum(grad_act_one * normed_one, 0)
    grad_gains = jnp.stack([grad_gain_one, grad_gain_two])
    grad_gains = butterfly(grad_gains, "fsdp")
    input_grad = low(grad_resid + norm_back(grad_act_one, normed_one, gain_one, inverse_one))
    rows_each = block // 2

    def down_rows(offset):
        return lambda other, step: (other * 2 + offset + step, 0)

    grad_down = placed(
        [
            (piece.reshape(2, rows_each, width), k, down_rows(0))
            for k, piece in enumerate(down_pieces)
        ],
        w_down.shape,
        (rows_each, width),
        write_rows,
    )
    gu_pieces, down_last, layer_out, input_grad, grad_down, part_out, grad_gains, part_qkv = (
        together(
            gu_pieces, down_last, layer_out, input_grad, grad_down, part_out, grad_gains, part_qkv
        )
    )
    gu_last = second_hop(gu_pieces)
    part_qkv = lax.all_gather(part_qkv, "ctx", axis=0)
    if strided:
        out_pieces = gathered(part_out, "ctx")
    else:
        out_pieces = [scatter_rows(gather_rows(part_out, "ctx"), "fsdp")]

    def gate_up_columns(offset):
        return lambda other, step: (other, 0, offset + step)

    grad_gate_up = placed(
        [(piece, k, gate_up_columns(0)) for k, piece in enumerate(gu_pieces)],
        w_gate_up.shape,
        (part, 2, hidden_own),
        write_pair,
    )
    grad_gate_up, gu_last, out_pieces, grad_gains = together(
        grad_gate_up, gu_last, out_pieces, grad_gains
    )
    grad_gains = butterfly(grad_gains, "ctx")
    grad_gains = lax.dynamic_slice_in_dim(grad_gains, lax.axis_index("fsdp") * shard, shard, 1)
    grad_gate_up = placed(
        [(piece, 3, gate_up_columns(k * fsdp_count // 2)) for k, piece in enumerate(gu_last)],
        w_gate_up.shape,
        (part, 2, hidden_own),
        write_pair,
        grad_gate_up,
    )
    grad_down = placed(
        [(piece[None], 3, down_rows(k)) for k, piece in enumerate(down_last)],
        w_down.shape,
        (rows_each, width),
        write_rows,
        grad_down,
    )
    if strided:
        grad_out = placed(
            [(piece[None], k, lambda other, step: (other, 0)) for k, piece in enumerate(out_pieces)],
            w_out.shape,
            out_pieces[0].shape,
            write_rows,
        )
    else:
        grad_out = out_pieces[0].astype(jnp.float32)
    if strided:
        grad_w_qkv = pl.pallas_call(
            functools.partial(write_heads, fsdp_count),
            grid=(3,),
            in_specs=[pl.BlockSpec((ctx_count, shard, own_width), lambda step: (0, 0, step))],
            out_specs=pl.BlockSpec((1, shard, width), lambda step: (step, 0, 0)),
            out_shape=jax.ShapeDtypeStruct((3, shard, width), jnp.float32),
            cost_estimate=pl.CostEstimate(
                flops=part_qkv.size, bytes_accessed=6 * part_qkv.size, transcendentals=0
            ),
        )(part_qkv)
        grad_w_qkv = jnp.transpose(grad_w_qkv, (1, 0, 2))
    else:
        part_qkv = jnp.transpose(part_qkv.reshape(ctx_count, shard, 3, own_width), (1, 2, 0, 3))
        grad_w_qkv = part_qkv.reshape(w_qkv.shape).astype(jnp.float32)
    return (
        layer_out[None],
        input_grad[None],
        grad_gains[0],
        grad_w_qkv,
        grad_out,
        grad_gains[1],
        grad_gate_up,
        grad_down,
    )


def solution(mesh):
    return jax.shard_map(
        per_device,
        mesh=mesh,
        in_specs=(
            P("fsdp", "ctx", None),
            P("fsdp", "ctx", None),
            P("fsdp", "ctx"),
            P("fsdp", None),
            P("fsdp"),
            P("fsdp", None, None),
            P("fsdp", None),
            P("fsdp"),
            P("fsdp", None, None),
            P("fsdp", None),
        ),
        out_specs=(
            P("fsdp", "ctx", None),
            P("fsdp", "ctx", None),
            P("fsdp"),
            P("fsdp", None, None),
            P("fsdp", None),
            P("fsdp"),
            P("fsdp", None, None),
            P("fsdp", None),
        ),
        check_vma=False,
    )
```

```python
import functools

import jax
import jax.numpy as jnp
from jax import lax
from jax.experimental import pallas as pl
from jax.experimental.pallas import tpu as pltpu
from jax.sharding import PartitionSpec as P

HD = 64

rope_theta = 130000.0
norm_eps = 1e-05
score_scale = 0.125
masked_score = -1e30
free = pl.CostEstimate(flops=1, bytes_accessed=1, transcendentals=0)


def swapped(array, axis, by):
    size = lax.axis_size(axis)
    return lax.ppermute(array, axis, [(i, i ^ by) for i in range(size)])


def gathered(array, axis):
    return [array] + [swapped(array, axis, k) for k in range(1, lax.axis_size(axis))]


def scattered(parts, axis):
    total = parts[0].astype(jnp.float32)
    for k in range(1, lax.axis_size(axis)):
        total = total + swapped(parts[k].astype(jnp.bfloat16), axis, k).astype(jnp.float32)
    return total


def paired(blocks):
    core = lax.axis_index("fsdp") % 2
    grid = blocks.reshape((blocks.shape[0] // 2, 2) + blocks.shape[1:])
    keep = lax.dynamic_index_in_dim(grid, core, 1, keepdims=False)
    got = swapped(lax.dynamic_index_in_dim(grid, 1 - core, 1, keepdims=False), "fsdp", 1)
    return jnp.stack([jnp.where(core == 0, keep, got), jnp.where(core == 0, got, keep)], 1)


def crossing(pairs):
    chip = lax.axis_index("fsdp") // 2
    return [
        lax.dynamic_index_in_dim(pairs, chip ^ k, 0, keepdims=False)
        for k in range(1, pairs.shape[0])
    ]


def crossed(sends, first=1):
    return [swapped(send, "fsdp", 2 * k) for k, send in enumerate(sends, first)]


def in_order(pairs, received):
    chip = lax.axis_index("fsdp") // 2
    for k, pair in enumerate(received, 1):
        pairs = lax.dynamic_update_index_in_dim(pairs, pair, chip ^ k, 0)
    return pairs.reshape((-1,) + pairs.shape[2:])


def first_hop(array):
    size = lax.axis_size("ctx")
    return [array] + [swapped(array, "ctx", k) for k in range(1, 3 if size == 4 else size)]


def second_hop(pieces):
    if lax.axis_size("ctx") != 4:
        return []
    half = pieces[0].shape[0] // 2
    return [swapped(pieces[1][:half], "ctx", 2), swapped(pieces[2][half:], "ctx", 1)]


def first_fold(parts):
    size = lax.axis_size("ctx")
    if size != 4:
        return [swapped(parts[k], "ctx", k) for k in range(1, size)]
    half = parts[0].shape[0] // 2
    return [swapped(parts[3][:half], "ctx", 1), swapped(parts[3][half:], "ctx", 2)]


def folded(parts, halves):
    if lax.axis_size("ctx") != 4:
        return []
    half = parts[0].shape[0] // 2
    over_x = jnp.concatenate([parts[1][:half], plus(parts[1][half:], halves[1])], 0)
    over_y = jnp.concatenate([plus(parts[2][:half], halves[0]), parts[2][half:]], 0)
    return [over_x, over_y]


def second_fold(sends, halves):
    if not sends:
        return halves
    return [swapped(sends[0], "ctx", 1), swapped(sends[1], "ctx", 2)]


def butterfly(array, axis):
    step = 1
    while step < lax.axis_size(axis):
        array = array + swapped(array, axis, step)
        step *= 2
    return array


def wide_fold(parts):
    size = lax.axis_size("ctx")
    if size != 4:
        return first_fold(parts)
    half = parts[0].shape[0] // 2
    return first_fold(parts) + [
        swapped(parts[1][:half], "ctx", 1),
        swapped(parts[2][half:], "ctx", 2),
    ]


def late_terms(parts, arrived):
    if lax.axis_size("ctx") != 4:
        return []
    half = parts[0].shape[0] // 2
    return [plus(parts[1][half:], arrived[1]), plus(parts[2][:half], arrived[0])]


def late_fold(terms):
    return [swapped(term, "ctx", k) for k, term in enumerate(terms, 1)]


def wide_sum(own, arrived, late):
    if not late:
        return plus(own, *arrived)
    half = own.shape[0] // 2
    return jnp.concatenate(
        [plus(own[:half], arrived[2], late[1]), plus(own[half:], arrived[3], late[0])], 0
    )


def plus(*terms):
    return low(sum(term.astype(jnp.float32) for term in terms))


def placed(pieces, shape, block, body, result=None):
    own = jnp.stack([lax.axis_index("ctx"), lax.axis_index("fsdp") // 2]).astype(jnp.int32)
    for piece, k, index in pieces:

        def out_map(step, own_ref, k=k, index=index):
            return index(own_ref[0] ^ k, own_ref[1], step)

        in_specs = [pl.BlockSpec((1,) + piece.shape[1:], lambda step, own_ref: (step, 0, 0))]
        operands = [own, piece]
        aliases = {}
        if result is not None:
            in_specs.append(pl.BlockSpec(memory_space=pl.ANY))
            operands.append(result)
            aliases = {2: 0}
        result = pl.pallas_call(
            body,
            grid_spec=pltpu.PrefetchScalarGridSpec(
                num_scalar_prefetch=1,
                grid=(piece.shape[0],),
                in_specs=in_specs,
                out_specs=pl.BlockSpec(block, out_map),
            ),
            out_shape=jax.ShapeDtypeStruct(shape, jnp.float32),
            input_output_aliases=aliases,
            cost_estimate=free,
        )(*operands)
    return result


def write_pair(own_ref, piece_ref, *refs):
    out_ref = refs[-1]
    half = piece_ref.shape[2] // 2
    out_ref[:, 0, :] = piece_ref[0, :, :half].astype(jnp.float32)
    out_ref[:, 1, :] = piece_ref[0, :, half:].astype(jnp.float32)


def write_rows(own_ref, piece_ref, *refs):
    refs[-1][...] = piece_ref[0].astype(jnp.float32)


def angles(positions, width):
    half_width = width // 2
    frequency = rope_theta ** (-2.0 * jnp.arange(half_width, dtype=jnp.float32) / width)
    phases = positions.astype(jnp.float32)[:, None] * frequency[None, :]
    return (jnp.cos(phases)[:, None, :], jnp.sin(phases)[:, None, :])


def rotate(values, cosine, sine):
    half_width = values.shape[-1] // 2
    leading = values[..., :half_width]
    trailing = values[..., half_width:]
    return jnp.concatenate(
        [leading * cosine - trailing * sine, trailing * cosine + leading * sine], -1
    )


def inverse_rms(values):
    return lax.rsqrt(jnp.mean(values * values, -1, keepdims=True) + norm_eps)


def norm_back(grad_normed, normed, gain, inverse):
    scaled = grad_normed * gain
    return inverse * (scaled - normed * jnp.mean(scaled * normed, -1, keepdims=True))


def product(left, right, left_dim, right_dim):
    return lax.dot_general(
        left, right, (((left_dim,), (right_dim,)), ((), ())), preferred_element_type=jnp.float32
    )


def low(values):
    return values.astype(jnp.bfloat16)


def together(*arrays):
    return lax.optimization_barrier(arrays)


def gather_rows(array, axis):
    return lax.all_gather(array, axis, axis=0, tiled=True)


def scatter_rows(array, axis):
    return lax.psum_scatter(low(array), axis, scatter_dimension=0, tiled=True)


def write_heads(groups, piece_ref, out_ref):
    count = piece_ref.shape[0]
    each = piece_ref.shape[2] // groups
    for group in range(groups):
        row = [
            piece_ref[index, :, group * each : (group + 1) * each].astype(jnp.float32)
            for index in range(count)
        ]
        out_ref[0, :, group * count * each : (group + 1) * count * each] = jnp.concatenate(row, 1)


def own_columns(own_ref, in_ref, out_ref):
    half = in_ref.shape[2]
    out_ref[0, :, :half] = in_ref[:, 0, :]
    out_ref[0, :, half:] = in_ref[:, 1, :]


def per_device(
    tokens, cotangent, block_ids, span_order, attn_gain, w_qkv, w_out, ffn_gain, w_gate_up, w_down
):
    ctx_count = lax.axis_size("ctx")
    fsdp_count = lax.axis_size("fsdp")
    ctx = lax.axis_index("ctx")
    rows = tokens.shape[1]
    width = tokens.shape[2]
    shard = w_qkv.shape[0]
    length = rows * ctx_count
    heads = width // HD // ctx_count
    own_width = heads * HD
    strided = (shard // HD) % ctx_count == 0

    chunks = jnp.bitwise_xor(ctx, jnp.arange(ctx_count, dtype=jnp.int32))
    order_row = span_order[0]
    spans = order_row.shape[0]
    half = length // spans
    local = jnp.arange(rows, dtype=jnp.int32)
    slots = (chunks[:, None] * (rows // half) + (local // half)[None, :]).reshape(length)
    matches = slots[:, None] == jnp.arange(spans, dtype=jnp.int32)[None, :]
    picked = jnp.sum(jnp.where(matches, order_row[None, :], 0), axis=1)
    positions = picked * half + jnp.tile(local % half, ctx_count)
    cosine, sine = angles(positions, HD)
    if strided:
        per = heads // fsdp_count
        qkv_own = lax.dynamic_index_in_dim(
            w_qkv.reshape(shard, 3, fsdp_count, ctx_count, per * HD), ctx, 3, keepdims=False
        ).reshape(shard, 3 * own_width)
        out_own = lax.dynamic_slice_in_dim(w_out, ctx * (per * HD), per * HD, 0)
        qkv_weight = gather_rows(qkv_own, "fsdp")
        out_weight = gather_rows(out_own, "fsdp")
    else:
        qkv_own = lax.dynamic_slice_in_dim(w_qkv, ctx * own_width, own_width, 2)
        qkv_weight = gather_rows(qkv_own.reshape(shard, 3 * own_width), "fsdp")
        out_weight = lax.dynamic_slice_in_dim(
            gather_rows(w_out, "fsdp"), ctx * own_width, own_width, 0
        )
    hidden_own = w_down.shape[0]
    part = shard // ctx_count
    gate_up_own = pl.pallas_call(
        own_columns,
        grid_spec=pltpu.PrefetchScalarGridSpec(
            num_scalar_prefetch=1,
            grid=(fsdp_count,),
            in_specs=[pl.BlockSpec((part, 2, hidden_own), lambda step, own: (own[0], 0, step))],
            out_specs=pl.BlockSpec((1, part, 2 * hidden_own), lambda step, own: (step, 0, 0)),
        ),
        out_shape=jax.ShapeDtypeStruct((fsdp_count, part, 2 * hidden_own), jnp.bfloat16),
        cost_estimate=free,
    )(ctx.astype(jnp.int32)[None], w_gate_up)
    gate_up_own = paired(gate_up_own)
    gate_up_sends = crossing(gate_up_own)
    gate_up_sends, gains, own_tokens = together(
        gate_up_sends, jnp.stack([attn_gain, ffn_gain]), tokens[0]
    )
    gate_up_mine = in_order(gate_up_own, crossed(gate_up_sends))
    gate_up_mine = gate_up_mine.reshape(fsdp_count * part, 2 * hidden_own)
    seq_inputs = jnp.concatenate(gathered(own_tokens, "ctx"), 0)
    gains = lax.all_gather(gains, "fsdp", axis=1, tiled=True).astype(jnp.float32)
    gain_one, gain_two = gains[0], gains[1]
    own_blocks, seq_inputs = together(block_ids[0], seq_inputs)
    blocks = jnp.concatenate(gathered(own_blocks, "ctx"), 0)
    allowed = (blocks[None, :] <= blocks[:, None])[None]
    gate_up_mine, qkv_weight = together(gate_up_mine, qkv_weight)
    gate_up_pieces = first_hop(gate_up_mine)

    def to_parts(array):
        lead = array.shape[:-1]
        array = array.reshape(lead + (fsdp_count, ctx_count, part))
        array = jnp.swapaxes(array, -3, -2).reshape(lead + (ctx_count, fsdp_count * part))
        return jnp.concatenate(
            [
                lax.dynamic_index_in_dim(array, ctx ^ k, array.ndim - 2, keepdims=False)
                for k in range(ctx_count)
            ],
            -1,
        )

    def from_parts(array):
        lead = array.shape[:-1]
        array = array.reshape(lead + (ctx_count, fsdp_count * part))
        array = jnp.stack(
            [
                lax.dynamic_index_in_dim(array, ctx ^ k, array.ndim - 2, keepdims=False)
                for k in range(ctx_count)
            ],
            -2,
        )
        array = array.reshape(lead + (ctx_count, fsdp_count, part))
        return jnp.swapaxes(array, -3, -2).reshape(lead + (width,))

    seq_inputs = seq_inputs.astype(jnp.float32)
    seq_inverse = inverse_rms(seq_inputs)
    seq_normed = seq_inputs * seq_inverse
    act_seq = low(seq_normed * gain_one)
    inputs, inverse_one, normed_one = seq_inputs[:rows], seq_inverse[:rows], seq_normed[:rows]
    qkv = product(act_seq, qkv_weight, 1, 0).reshape(length, 3, heads, HD)
    query = low(rotate(qkv[:, 0], cosine, sine))
    keys = low(rotate(qkv[:, 1], cosine, sine))
    values = low(qkv[:, 2])
    scores = (
        jnp.einsum("qhe,khe->hqk", query, keys, preferred_element_type=jnp.float32) * score_scale
    )
    scores = jnp.where(allowed, scores, masked_score)
    top = jnp.max(scores, -1, keepdims=True)
    weights = jnp.where(allowed, jnp.exp(scores - top), 0.0)
    total = jnp.sum(weights, -1, keepdims=True)
    probs = weights / total
    probs_b = low(probs)
    attended = jnp.einsum("hqk,khe->qhe", probs_b, values, preferred_element_type=jnp.float32)
    attn_b = low(attended).reshape(length, own_width)
    branch = product(attn_b, out_weight, 1, 0).reshape(ctx_count, rows, width)
    resid = inputs + scattered([branch[k] for k in range(ctx_count)], "ctx")

    inverse_two = inverse_rms(resid)
    normed_two = resid * inverse_two
    act_two = to_parts(low(normed_two * gain_two))
    cot = gather_rows(cotangent[0], "fsdp")
    act_two, cot, gate_up_pieces = together(act_two, cot, gate_up_pieces)
    act_two = gather_rows(act_two, "fsdp")
    gate_up_weight = jnp.concatenate(gate_up_pieces + second_hop(gate_up_pieces), 0)
    gate_up = product(act_two, gate_up_weight, 1, 0)
    gate = gate_up[:, :hidden_own]
    upward = gate_up[:, hidden_own:]
    sigma = jax.nn.sigmoid(gate)
    swish = gate * sigma
    hidden = low(swish * upward)
    block = hidden_own // ctx_count
    grad_hidden = product(cot, w_down, 1, 1)
    grad_gate = grad_hidden * upward * sigma * (1.0 + gate * (1.0 - sigma))
    grad_up = grad_hidden * swish
    grad_gu = low(jnp.concatenate([grad_gate, grad_up], 1))
    span = fsdp_count * part

    def gu_term(k):
        return low(product(act_two[:, k * span : (k + 1) * span], grad_gu, 0, 0))

    grad_act_two = low(product(grad_gu, gate_up_weight, 1, 1))
    gu_final = gu_term(ctx_count - 1)
    grad_act_two, grad_gu, gu_final = together(grad_act_two, grad_gu, gu_final)
    grad_act_two = scatter_rows(grad_act_two, "fsdp")
    part_gu = [gu_term(k) for k in range(ctx_count - 1)] + [gu_final]
    gu_arrived = wide_fold(part_gu)
    out_part = low(product(hidden, w_down, 1, 0))
    part_down = low(product(hidden, cot, 0, 0)).reshape(ctx_count, block, width)
    part_down = [
        lax.dynamic_index_in_dim(part_down, ctx ^ k, 0, keepdims=False) for k in range(ctx_count)
    ]
    part_gu, gu_arrived, out_part, part_down = together(part_gu, gu_arrived, out_part, part_down)
    gu_terms = late_terms(part_gu, gu_arrived)
    grad_act_two, out_part = together(grad_act_two, out_part)
    gu_late = late_fold(gu_terms)
    layer_part = scatter_rows(out_part, "fsdp")
    grad_act_two = from_parts(grad_act_two).astype(jnp.float32)
    grad_gain_two = jnp.sum(grad_act_two * normed_two, 0)
    grad_resid = cotangent[0].astype(jnp.float32) + norm_back(
        grad_act_two, normed_two, gain_two, inverse_two
    )

    grad_branch = jnp.concatenate(gathered(low(grad_resid), "ctx"), 0)
    grad_branch, gu_late, part_down = together(grad_branch, gu_late, part_down)
    down_halves = first_fold(part_down)
    gu_sum = wide_sum(part_gu[0], gu_arrived, gu_late)
    gu_pairs = paired(gu_sum.reshape(fsdp_count, part, 2 * hidden_own))
    part_out = low(product(attn_b, grad_branch, 0, 0))
    grad_att = low(product(grad_branch, out_weight, 1, 1)).reshape(length, heads, HD)
    gu_sends = crossing(gu_pairs)
    grad_att, part_out, gu_pairs, gu_sends, down_halves = together(
        grad_att, part_out, gu_pairs, gu_sends, down_halves
    )
    gu_received = crossed(gu_sends)
    down_last = second_fold(folded(part_down, down_halves), down_halves)
    part_out = scatter_rows(part_out, "fsdp") if strided else part_out
    delta = jnp.sum(grad_att.astype(jnp.float32) * attended, -1)
    grad_probs = jnp.einsum("qhe,khe->hqk", grad_att, values, preferred_element_type=jnp.float32)
    grad_scores = low(probs * (grad_probs - delta.T[..., None]))
    grad_scores, gu_received[:1] = together(grad_scores, gu_received[:1])
    grad_values = jnp.einsum("hqk,qhe->khe", probs_b, grad_att, preferred_element_type=jnp.float32)
    grad_query = (
        jnp.einsum("hqk,khe->qhe", grad_scores, keys, preferred_element_type=jnp.float32)
        * score_scale
    )
    grad_keys = (
        jnp.einsum("hqk,qhe->khe", grad_scores, query, preferred_element_type=jnp.float32)
        * score_scale
    )
    grad_qkv = low(
        jnp.stack(
            [rotate(grad_query, cosine, -sine), rotate(grad_keys, cosine, -sine), grad_values], 1
        )
    ).reshape(length, 3 * own_width)
    grad_qkv, down_last, layer_part, gu_received[::2] = together(
        grad_qkv, down_last, layer_part, gu_received[::2]
    )

    gu_own = lax.dynamic_index_in_dim(gu_pairs, lax.axis_index("fsdp") // 2, 0, keepdims=False)
    chips = len(gu_received) + 1
    gu_near = first_hop(jnp.concatenate([gu_own] + gu_received[: chips // 2 - 1], 0))
    part_qkv = low(product(act_seq, grad_qkv, 0, 0))
    back = low(product(grad_qkv, qkv_weight, 1, 1))
    grad_gain_one = jnp.sum(back.astype(jnp.float32) * seq_normed, 0)
    grad_gains = jnp.stack([grad_gain_one, grad_gain_two])
    back = back.reshape(ctx_count, rows, width)
    back = [back[k] for k in range(ctx_count)]
    part_down = plus(part_down[0], *down_last)
    part_qkv, part_out, back, gu_near, gu_received, grad_gains, part_down = together(
        part_qkv, part_out, back, gu_near, gu_received, grad_gains, part_down
    )
    part_qkv = scatter_rows(part_qkv, "fsdp")
    back_halves = first_fold(back)
    grad_gains, back_halves = together(grad_gains, back_halves)
    gu_far = first_hop(jnp.concatenate(gu_received[chips // 2 - 1 :], 0))
    back_last = second_fold(folded(back, back_halves), back_halves)
    grad_act_one = sum(term.astype(jnp.float32) for term in [back[0]] + back_last)
    if ctx_count == 4:
        gu_near.append(swapped(gu_near[1], "ctx", 2))
    layer_out = low(resid + layer_part.astype(jnp.float32))
    input_grad = low(grad_resid + norm_back(grad_act_one, normed_one, gain_one, inverse_one))

    def gate_up_columns(offset):
        return lambda other, chip, step: (other, 0, 2 * (chip ^ (offset + step // 2)) + step % 2)

    grad_gate_up = placed(
        [(piece, k, gate_up_columns(0)) for k, piece in enumerate(gu_near[:3])],
        w_gate_up.shape,
        (part, 2, hidden_own),
        write_pair,
    )
    gu_far, gu_near, layer_out, input_grad, part_down, grad_gains, grad_gate_up = together(
        gu_far, gu_near, layer_out, input_grad, part_down, grad_gains, grad_gate_up
    )
    if ctx_count == 4:
        gu_far.append(swapped(gu_far[2], "ctx", 1))
    down_pieces = first_hop(part_down)
    grad_gains = butterfly(grad_gains, "fsdp")
    grad_gate_up = placed(
        [(piece, k, gate_up_columns(0)) for k, piece in enumerate(gu_near) if k > 2]
        + [(piece, k, gate_up_columns(chips // 2)) for k, piece in enumerate(gu_far[:3])],
        w_gate_up.shape,
        (part, 2, hidden_own),
        write_pair,
        grad_gate_up,
    )
    gu_far, down_pieces, grad_gate_up, part_qkv = together(
        gu_far, down_pieces, grad_gate_up, part_qkv
    )
    part_qkv = lax.all_gather(part_qkv, "ctx", axis=0)
    down_last = second_hop(down_pieces)
    if strided:
        out_pieces = gathered(part_out, "ctx")
    else:
        out_pieces = [scatter_rows(gather_rows(part_out, "ctx"), "fsdp")]
    grad_gains = butterfly(grad_gains, "ctx")
    grad_gains = lax.dynamic_slice_in_dim(grad_gains, lax.axis_index("fsdp") * shard, shard, 1)
    grad_gate_up = placed(
        [(piece, k, gate_up_columns(chips // 2)) for k, piece in enumerate(gu_far) if k > 2],
        w_gate_up.shape,
        (part, 2, hidden_own),
        write_pair,
        grad_gate_up,
    )
    rows_each = block // 2

    def down_rows(offset):
        return lambda other, chip, step: (other * 2 + offset + step, 0)

    grad_down = placed(
        [
            (piece.reshape(2, rows_each, width), k, down_rows(0))
            for k, piece in enumerate(down_pieces)
        ]
        + [(piece[None], 3, down_rows(k)) for k, piece in enumerate(down_last)],
        w_down.shape,
        (rows_each, width),
        write_rows,
    )
    if strided:
        grad_out = placed(
            [
                (piece[None], k, lambda other, chip, step: (other, 0))
                for k, piece in enumerate(out_pieces)
            ],
            w_out.shape,
            out_pieces[0].shape,
            write_rows,
        )
    else:
        grad_out = out_pieces[0].astype(jnp.float32)
    if strided:
        grad_w_qkv = pl.pallas_call(
            functools.partial(write_heads, fsdp_count),
            grid=(3,),
            in_specs=[pl.BlockSpec((ctx_count, shard, own_width), lambda step: (0, 0, step))],
            out_specs=pl.BlockSpec((1, shard, width), lambda step: (step, 0, 0)),
            out_shape=jax.ShapeDtypeStruct((3, shard, width), jnp.float32),
            cost_estimate=free,
        )(part_qkv)
        grad_w_qkv = jnp.transpose(grad_w_qkv, (1, 0, 2))
    else:
        part_qkv = jnp.transpose(part_qkv.reshape(ctx_count, shard, 3, own_width), (1, 2, 0, 3))
        grad_w_qkv = part_qkv.reshape(w_qkv.shape).astype(jnp.float32)
    return (
        layer_out[None],
        input_grad[None],
        grad_gains[0],
        grad_w_qkv,
        grad_out,
        grad_gains[1],
        grad_gate_up,
        grad_down,
    )


def solution(mesh):
    return jax.shard_map(
        per_device,
        mesh=mesh,
        in_specs=(
            P("fsdp", "ctx", None),
            P("fsdp", "ctx", None),
            P("fsdp", "ctx"),
            P("fsdp", None),
            P("fsdp"),
            P("fsdp", None, None),
            P("fsdp", None),
            P("fsdp"),
            P("fsdp", None, None),
            P("fsdp", None),
        ),
        out_specs=(
            P("fsdp", "ctx", None),
            P("fsdp", "ctx", None),
            P("fsdp"),
            P("fsdp", None, None),
            P("fsdp", None),
            P("fsdp"),
            P("fsdp", None, None),
            P("fsdp", None),
        ),
        check_vma=False,
    )
```

```python
import functools

import jax
import jax.numpy as jnp
from jax import lax
from jax.experimental import pallas as pl
from jax.experimental.pallas import tpu as pltpu
from jax.sharding import PartitionSpec as P

HD = 64

rope_theta = 130000.0
norm_eps = 1e-05
score_scale = 0.125
masked_score = -1e30
free = pl.CostEstimate(flops=1, bytes_accessed=1, transcendentals=0)


def swapped(array, axis, by):
    size = lax.axis_size(axis)
    return lax.ppermute(array, axis, [(i, i ^ by) for i in range(size)])


def gathered(array, axis):
    return [array] + [swapped(array, axis, k) for k in range(1, lax.axis_size(axis))]


def scattered(parts, axis):
    total = parts[0].astype(jnp.float32)
    for k in range(1, lax.axis_size(axis)):
        total = total + swapped(parts[k].astype(jnp.bfloat16), axis, k).astype(jnp.float32)
    return total


def paired(blocks):
    core = lax.axis_index("fsdp") % 2
    grid = blocks.reshape((blocks.shape[0] // 2, 2) + blocks.shape[1:])
    keep = lax.dynamic_index_in_dim(grid, core, 1, keepdims=False)
    got = swapped(lax.dynamic_index_in_dim(grid, 1 - core, 1, keepdims=False), "fsdp", 1)
    return jnp.stack([jnp.where(core == 0, keep, got), jnp.where(core == 0, got, keep)], 1)


def crossing(pairs):
    chip = lax.axis_index("fsdp") // 2
    return [
        lax.dynamic_index_in_dim(pairs, chip ^ k, 0, keepdims=False)
        for k in range(1, pairs.shape[0])
    ]


def crossed(sends, first=1):
    return [swapped(send, "fsdp", 2 * k) for k, send in enumerate(sends, first)]


def in_order(pairs, received):
    chip = lax.axis_index("fsdp") // 2
    for k, pair in enumerate(received, 1):
        pairs = lax.dynamic_update_index_in_dim(pairs, pair, chip ^ k, 0)
    return pairs.reshape((-1,) + pairs.shape[2:])


def first_hop(array):
    size = lax.axis_size("ctx")
    return [array] + [swapped(array, "ctx", k) for k in range(1, 3 if size == 4 else size)]


def second_hop(pieces):
    if lax.axis_size("ctx") != 4:
        return []
    half = pieces[0].shape[0] // 2
    return [swapped(pieces[1][:half], "ctx", 2), swapped(pieces[2][half:], "ctx", 1)]


def first_fold(parts):
    size = lax.axis_size("ctx")
    if size != 4:
        return [swapped(parts[k], "ctx", k) for k in range(1, size)]
    half = parts[0].shape[0] // 2
    return [swapped(parts[3][:half], "ctx", 1), swapped(parts[3][half:], "ctx", 2)]


def folded(parts, halves):
    if lax.axis_size("ctx") != 4:
        return []
    half = parts[0].shape[0] // 2
    over_x = jnp.concatenate([parts[1][:half], plus(parts[1][half:], halves[1])], 0)
    over_y = jnp.concatenate([plus(parts[2][:half], halves[0]), parts[2][half:]], 0)
    return [over_x, over_y]


def second_fold(sends, halves):
    if not sends:
        return halves
    return [swapped(sends[0], "ctx", 1), swapped(sends[1], "ctx", 2)]


def butterfly(array, axis):
    step = 1
    while step < lax.axis_size(axis):
        array = array + swapped(array, axis, step)
        step *= 2
    return array


def wide_fold(parts):
    size = lax.axis_size("ctx")
    if size != 4:
        return first_fold(parts)
    half = parts[0].shape[0] // 2
    return first_fold(parts) + [
        swapped(parts[1][:half], "ctx", 1),
        swapped(parts[2][half:], "ctx", 2),
    ]


def late_terms(parts, arrived):
    if lax.axis_size("ctx") != 4:
        return []
    half = parts[0].shape[0] // 2
    return [plus(parts[1][half:], arrived[1]), plus(parts[2][:half], arrived[0])]


def late_fold(terms):
    return [swapped(term, "ctx", k) for k, term in enumerate(terms, 1)]


def wide_sum(own, arrived, late):
    if not late:
        return plus(own, *arrived)
    half = own.shape[0] // 2
    return jnp.concatenate(
        [plus(own[:half], arrived[2], late[1]), plus(own[half:], arrived[3], late[0])], 0
    )


def plus(*terms):
    return low(sum(term.astype(jnp.float32) for term in terms))


def placed(pieces, shape, block, body, result=None):
    own = jnp.stack([lax.axis_index("ctx"), lax.axis_index("fsdp") // 2]).astype(jnp.int32)
    for piece, k, index in pieces:

        def out_map(step, own_ref, k=k, index=index):
            return index(own_ref[0] ^ k, own_ref[1], step)

        in_specs = [pl.BlockSpec((1,) + piece.shape[1:], lambda step, own_ref: (step, 0, 0))]
        operands = [own, piece]
        aliases = {}
        if result is not None:
            in_specs.append(pl.BlockSpec(memory_space=pl.ANY))
            operands.append(result)
            aliases = {2: 0}
        result = pl.pallas_call(
            body,
            grid_spec=pltpu.PrefetchScalarGridSpec(
                num_scalar_prefetch=1,
                grid=(piece.shape[0],),
                in_specs=in_specs,
                out_specs=pl.BlockSpec(block, out_map),
            ),
            out_shape=jax.ShapeDtypeStruct(shape, jnp.float32),
            input_output_aliases=aliases,
            cost_estimate=free,
        )(*operands)
    return result


def write_pair(own_ref, piece_ref, *refs):
    out_ref = refs[-1]
    half = piece_ref.shape[2] // 2
    out_ref[:, 0, :] = piece_ref[0, :, :half].astype(jnp.float32)
    out_ref[:, 1, :] = piece_ref[0, :, half:].astype(jnp.float32)


def write_rows(own_ref, piece_ref, *refs):
    refs[-1][...] = piece_ref[0].astype(jnp.float32)


def stacked(pieces, shape):
    own = lax.axis_index("ctx").astype(jnp.int32)[None]
    each = shape[0] // lax.axis_size("ctx")

    def body(own_ref, *refs):
        for ref, (piece, k, row) in zip(refs, pieces):
            start = pl.multiple_of((own_ref[0] ^ k) * each + row, 16)
            refs[-1][pl.ds(start, piece.shape[0]), :] = ref[...].astype(jnp.float32)

    return pl.pallas_call(
        body,
        grid_spec=pltpu.PrefetchScalarGridSpec(
            num_scalar_prefetch=1,
            grid=(1,),
            in_specs=[
                pl.BlockSpec(piece.shape, lambda step, own_ref: (0, 0)) for piece, _, _ in pieces
            ],
            out_specs=pl.BlockSpec(shape, lambda step, own_ref: (0, 0)),
        ),
        out_shape=jax.ShapeDtypeStruct(shape, jnp.float32),
        cost_estimate=free,
    )(own, *[piece for piece, _, _ in pieces])


def angles(positions, width):
    half_width = width // 2
    frequency = rope_theta ** (-2.0 * jnp.arange(half_width, dtype=jnp.float32) / width)
    phases = positions.astype(jnp.float32)[:, None] * frequency[None, :]
    return (jnp.cos(phases)[:, None, :], jnp.sin(phases)[:, None, :])


def rotate(values, cosine, sine):
    half_width = values.shape[-1] // 2
    leading = values[..., :half_width]
    trailing = values[..., half_width:]
    return jnp.concatenate(
        [leading * cosine - trailing * sine, trailing * cosine + leading * sine], -1
    )


def inverse_rms(values):
    return lax.rsqrt(jnp.mean(values * values, -1, keepdims=True) + norm_eps)


def norm_back(grad_normed, normed, gain, inverse):
    scaled = grad_normed * gain
    return inverse * (scaled - normed * jnp.mean(scaled * normed, -1, keepdims=True))


def product(left, right, left_dim, right_dim):
    return lax.dot_general(
        left, right, (((left_dim,), (right_dim,)), ((), ())), preferred_element_type=jnp.float32
    )


def low(values):
    return values.astype(jnp.bfloat16)


def together(*arrays):
    return lax.optimization_barrier(arrays)


def gather_rows(array, axis):
    return lax.all_gather(array, axis, axis=0, tiled=True)


def scatter_rows(array, axis):
    return lax.psum_scatter(low(array), axis, scatter_dimension=0, tiled=True)


def write_heads(groups, piece_ref, out_ref):
    count = piece_ref.shape[0]
    each = piece_ref.shape[2] // groups
    for group in range(groups):
        row = [
            piece_ref[index, :, group * each : (group + 1) * each].astype(jnp.float32)
            for index in range(count)
        ]
        out_ref[0, :, group * count * each : (group + 1) * count * each] = jnp.concatenate(row, 1)


def own_columns(own_ref, in_ref, out_ref):
    half = in_ref.shape[2]
    out_ref[0, :, :half] = in_ref[:, 0, :]
    out_ref[0, :, half:] = in_ref[:, 1, :]


def per_device(
    tokens, cotangent, block_ids, span_order, attn_gain, w_qkv, w_out, ffn_gain, w_gate_up, w_down
):
    ctx_count = lax.axis_size("ctx")
    fsdp_count = lax.axis_size("fsdp")
    ctx = lax.axis_index("ctx")
    rows = tokens.shape[1]
    width = tokens.shape[2]
    shard = w_qkv.shape[0]
    length = rows * ctx_count
    heads = width // HD // ctx_count
    own_width = heads * HD
    strided = (shard // HD) % ctx_count == 0

    chunks = jnp.bitwise_xor(ctx, jnp.arange(ctx_count, dtype=jnp.int32))
    order_row = span_order[0]
    spans = order_row.shape[0]
    half = length // spans
    local = jnp.arange(rows, dtype=jnp.int32)
    slots = (chunks[:, None] * (rows // half) + (local // half)[None, :]).reshape(length)
    matches = slots[:, None] == jnp.arange(spans, dtype=jnp.int32)[None, :]
    picked = jnp.sum(jnp.where(matches, order_row[None, :], 0), axis=1)
    positions = picked * half + jnp.tile(local % half, ctx_count)
    cosine, sine = angles(positions, HD)
    if strided:
        per = heads // fsdp_count
        qkv_own = lax.dynamic_index_in_dim(
            w_qkv.reshape(shard, 3, fsdp_count, ctx_count, per * HD), ctx, 3, keepdims=False
        ).reshape(shard, 3 * own_width)
        out_own = lax.dynamic_slice_in_dim(w_out, ctx * (per * HD), per * HD, 0)
        qkv_weight = gather_rows(qkv_own, "fsdp")
        out_weight = gather_rows(out_own, "fsdp")
    else:
        qkv_own = lax.dynamic_slice_in_dim(w_qkv, ctx * own_width, own_width, 2)
        qkv_weight = gather_rows(qkv_own.reshape(shard, 3 * own_width), "fsdp")
        out_weight = lax.dynamic_slice_in_dim(
            gather_rows(w_out, "fsdp"), ctx * own_width, own_width, 0
        )
    hidden_own = w_down.shape[0]
    part = shard // ctx_count
    gate_up_own = pl.pallas_call(
        own_columns,
        grid_spec=pltpu.PrefetchScalarGridSpec(
            num_scalar_prefetch=1,
            grid=(fsdp_count,),
            in_specs=[pl.BlockSpec((part, 2, hidden_own), lambda step, own: (own[0], 0, step))],
            out_specs=pl.BlockSpec((1, part, 2 * hidden_own), lambda step, own: (step, 0, 0)),
        ),
        out_shape=jax.ShapeDtypeStruct((fsdp_count, part, 2 * hidden_own), jnp.bfloat16),
        cost_estimate=free,
    )(ctx.astype(jnp.int32)[None], w_gate_up)
    gate_up_own = paired(gate_up_own)
    gate_up_sends = crossing(gate_up_own)
    gate_up_sends, gains, own_tokens = together(
        gate_up_sends, jnp.stack([attn_gain, ffn_gain]), tokens[0]
    )
    gate_up_mine = in_order(gate_up_own, crossed(gate_up_sends))
    gate_up_mine = gate_up_mine.reshape(fsdp_count * part, 2 * hidden_own)
    seq_inputs = jnp.concatenate(gathered(own_tokens, "ctx"), 0)
    gains = lax.all_gather(gains, "fsdp", axis=1, tiled=True).astype(jnp.float32)
    gain_one, gain_two = gains[0], gains[1]
    own_blocks, seq_inputs = together(block_ids[0], seq_inputs)
    blocks = jnp.concatenate(gathered(own_blocks, "ctx"), 0)
    allowed = (blocks[None, :] <= blocks[:, None])[None]
    gate_up_mine, qkv_weight = together(gate_up_mine, qkv_weight)
    gate_up_pieces = first_hop(gate_up_mine)

    def to_parts(array):
        lead = array.shape[:-1]
        array = array.reshape(lead + (fsdp_count, ctx_count, part))
        array = jnp.swapaxes(array, -3, -2).reshape(lead + (ctx_count, fsdp_count * part))
        return jnp.concatenate(
            [
                lax.dynamic_index_in_dim(array, ctx ^ k, array.ndim - 2, keepdims=False)
                for k in range(ctx_count)
            ],
            -1,
        )

    def from_parts(array):
        lead = array.shape[:-1]
        array = array.reshape(lead + (ctx_count, fsdp_count * part))
        array = jnp.stack(
            [
                lax.dynamic_index_in_dim(array, ctx ^ k, array.ndim - 2, keepdims=False)
                for k in range(ctx_count)
            ],
            -2,
        )
        array = array.reshape(lead + (ctx_count, fsdp_count, part))
        return jnp.swapaxes(array, -3, -2).reshape(lead + (width,))

    seq_inputs = seq_inputs.astype(jnp.float32)
    seq_inverse = inverse_rms(seq_inputs)
    seq_normed = seq_inputs * seq_inverse
    act_seq = low(seq_normed * gain_one)
    inputs, inverse_one, normed_one = seq_inputs[:rows], seq_inverse[:rows], seq_normed[:rows]
    qkv = product(act_seq, qkv_weight, 1, 0).reshape(length, 3, heads, HD)
    query = low(rotate(qkv[:, 0], cosine, sine))
    keys = low(rotate(qkv[:, 1], cosine, sine))
    values = low(qkv[:, 2])
    scores = (
        jnp.einsum("qhe,khe->hqk", query, keys, preferred_element_type=jnp.float32) * score_scale
    )
    scores = jnp.where(allowed, scores, masked_score)
    top = jnp.max(scores, -1, keepdims=True)
    weights = jnp.where(allowed, jnp.exp(scores - top), 0.0)
    total = jnp.sum(weights, -1, keepdims=True)
    probs = weights / total
    probs_b = low(probs)
    attended = jnp.einsum("hqk,khe->qhe", probs_b, values, preferred_element_type=jnp.float32)
    attn_b = low(attended).reshape(length, own_width)
    branch = product(attn_b, out_weight, 1, 0).reshape(ctx_count, rows, width)
    resid = inputs + scattered([branch[k] for k in range(ctx_count)], "ctx")

    inverse_two = inverse_rms(resid)
    normed_two = resid * inverse_two
    act_two = to_parts(low(normed_two * gain_two))
    cot = gather_rows(cotangent[0], "fsdp")
    act_two, cot, gate_up_pieces = together(act_two, cot, gate_up_pieces)
    act_two = gather_rows(act_two, "fsdp")
    gate_up_weight = jnp.concatenate(gate_up_pieces + second_hop(gate_up_pieces), 0)
    gate_up = product(act_two, gate_up_weight, 1, 0)
    gate = gate_up[:, :hidden_own]
    upward = gate_up[:, hidden_own:]
    sigma = jax.nn.sigmoid(gate)
    swish = gate * sigma
    hidden = low(swish * upward)
    block = hidden_own // ctx_count
    grad_hidden = product(cot, w_down, 1, 1)
    grad_gate = grad_hidden * upward * sigma * (1.0 + gate * (1.0 - sigma))
    grad_up = grad_hidden * swish
    grad_gu = low(jnp.concatenate([grad_gate, grad_up], 1))
    span = fsdp_count * part

    def gu_term(k):
        return low(product(act_two[:, k * span : (k + 1) * span], grad_gu, 0, 0))

    grad_act_two = low(product(grad_gu, gate_up_weight, 1, 1))
    gu_final = gu_term(ctx_count - 1)
    grad_act_two, grad_gu, gu_final = together(grad_act_two, grad_gu, gu_final)
    grad_act_two = scatter_rows(grad_act_two, "fsdp")
    part_gu = [gu_term(k) for k in range(ctx_count - 1)] + [gu_final]
    gu_arrived = wide_fold(part_gu)
    out_part = low(product(hidden, w_down, 1, 0))
    part_down = low(product(hidden, cot, 0, 0)).reshape(ctx_count, block, width)
    part_down = [
        lax.dynamic_index_in_dim(part_down, ctx ^ k, 0, keepdims=False) for k in range(ctx_count)
    ]
    part_gu, gu_arrived, out_part, part_down = together(part_gu, gu_arrived, out_part, part_down)
    gu_terms = late_terms(part_gu, gu_arrived)
    grad_act_two, out_part = together(grad_act_two, out_part)
    gu_late = late_fold(gu_terms)
    layer_part = scatter_rows(out_part, "fsdp")
    grad_act_two = from_parts(grad_act_two).astype(jnp.float32)
    grad_gain_two = jnp.sum(grad_act_two * normed_two, 0)
    grad_resid = cotangent[0].astype(jnp.float32) + norm_back(
        grad_act_two, normed_two, gain_two, inverse_two
    )

    grad_branch = jnp.concatenate(gathered(low(grad_resid), "ctx"), 0)
    grad_branch, gu_late, part_down = together(grad_branch, gu_late, part_down)
    down_halves = first_fold(part_down)
    gu_sum = wide_sum(part_gu[0], gu_arrived, gu_late)
    gu_pairs = paired(gu_sum.reshape(fsdp_count, part, 2 * hidden_own))
    part_out = low(product(attn_b, grad_branch, 0, 0))
    grad_att = low(product(grad_branch, out_weight, 1, 1)).reshape(length, heads, HD)
    gu_sends = crossing(gu_pairs)
    grad_att, part_out, gu_pairs, gu_sends, down_halves = together(
        grad_att, part_out, gu_pairs, gu_sends, down_halves
    )
    gu_received = crossed(gu_sends)
    down_last = second_fold(folded(part_down, down_halves), down_halves)
    part_out = scatter_rows(part_out, "fsdp") if strided else part_out
    delta = jnp.sum(grad_att.astype(jnp.float32) * attended, -1)
    grad_probs = jnp.einsum("qhe,khe->hqk", grad_att, values, preferred_element_type=jnp.float32)
    grad_scores = low(probs * (grad_probs - delta.T[..., None]))
    grad_scores, gu_received[:1] = together(grad_scores, gu_received[:1])
    gu_own = lax.dynamic_index_in_dim(gu_pairs, lax.axis_index("fsdp") // 2, 0, keepdims=False)
    chips = len(gu_received) + 1
    gu_near = first_hop(jnp.concatenate([gu_own] + gu_received[: chips // 2 - 1], 0))
    grad_values = jnp.einsum("hqk,qhe->khe", probs_b, grad_att, preferred_element_type=jnp.float32)
    grad_query = (
        jnp.einsum("hqk,khe->qhe", grad_scores, keys, preferred_element_type=jnp.float32)
        * score_scale
    )
    grad_keys = (
        jnp.einsum("hqk,qhe->khe", grad_scores, query, preferred_element_type=jnp.float32)
        * score_scale
    )
    grad_qkv = low(
        jnp.stack(
            [rotate(grad_query, cosine, -sine), rotate(grad_keys, cosine, -sine), grad_values], 1
        )
    ).reshape(length, 3 * own_width)
    part_qkv = low(product(act_seq, grad_qkv, 0, 0))
    back = low(product(grad_qkv, qkv_weight, 1, 1))
    grad_gain_one = jnp.sum(back.astype(jnp.float32) * seq_normed, 0)
    grad_gains = jnp.stack([grad_gain_one, grad_gain_two])
    back = back.reshape(ctx_count, rows, width)
    back = [back[k] for k in range(ctx_count)]
    part_qkv, back, grad_gains, down_last, layer_part, gu_received[::2], gu_near = together(
        part_qkv, back, grad_gains, down_last, layer_part, gu_received[::2], gu_near
    )

    back_halves = first_fold(back)
    down_pieces = first_hop(plus(part_down[0], *down_last))
    part_qkv, part_out, back_halves, gu_received, down_pieces = together(
        part_qkv, part_out, back_halves, gu_received, down_pieces
    )
    part_qkv = scatter_rows(part_qkv, "fsdp")
    gu_far = first_hop(jnp.concatenate(gu_received[chips // 2 - 1 :], 0))
    back_last = second_fold(folded(back, back_halves), back_halves)
    grad_act_one = sum(term.astype(jnp.float32) for term in [back[0]] + back_last)
    if ctx_count == 4:
        gu_near.append(swapped(gu_near[1], "ctx", 2))
    grad_act_one, gu_near[:3] = together(grad_act_one, gu_near[:3])
    layer_out = low(resid + layer_part.astype(jnp.float32))
    input_grad = low(grad_resid + norm_back(grad_act_one, normed_one, gain_one, inverse_one))

    def gate_up_columns(offset):
        return lambda other, chip, step: (other, 0, 2 * (chip ^ (offset + step // 2)) + step % 2)

    grad_gate_up = placed(
        [(piece, k, gate_up_columns(0)) for k, piece in enumerate(gu_near[:3])],
        w_gate_up.shape,
        (part, 2, hidden_own),
        write_pair,
    )
    gu_far, gu_near, layer_out, input_grad, down_pieces, grad_gate_up, part_qkv = together(
        gu_far, gu_near, layer_out, input_grad, down_pieces, grad_gate_up, part_qkv
    )
    part_qkv = lax.all_gather(part_qkv, "ctx", axis=0)
    if ctx_count == 4:
        gu_far.append(swapped(gu_far[2], "ctx", 1))
    down_last = second_hop(down_pieces)
    grad_gate_up = placed(
        [(piece, k, gate_up_columns(0)) for k, piece in enumerate(gu_near) if k > 2]
        + [(piece, k, gate_up_columns(chips // 2)) for k, piece in enumerate(gu_far[:3])],
        w_gate_up.shape,
        (part, 2, hidden_own),
        write_pair,
        grad_gate_up,
    )
    rows_each = block // 2

    def down_rows(offset):
        return lambda other, chip, step: (other * 2 + offset + step, 0)

    grad_down = placed(
        [
            (piece.reshape(2, rows_each, width), k, down_rows(0))
            for k, piece in enumerate(down_pieces)
        ],
        w_down.shape,
        (rows_each, width),
        write_rows,
    )
    grad_gate_up, grad_down, grad_gains = together(grad_gate_up, grad_down, grad_gains)
    grad_gains = butterfly(grad_gains, "fsdp")
    gu_far, down_last, grad_gate_up, grad_down, grad_gains = together(
        gu_far, down_last, grad_gate_up, grad_down, grad_gains
    )
    if strided:
        out_pieces = gathered(part_out, "ctx")
    else:
        out_pieces = [scatter_rows(gather_rows(part_out, "ctx"), "fsdp")]
    grad_gate_up = placed(
        [(piece, k, gate_up_columns(chips // 2)) for k, piece in enumerate(gu_far) if k > 2],
        w_gate_up.shape,
        (part, 2, hidden_own),
        write_pair,
        grad_gate_up,
    )
    grad_down = placed(
        [(piece[None], 3, down_rows(k)) for k, piece in enumerate(down_last)],
        w_down.shape,
        (rows_each, width),
        write_rows,
        grad_down,
    )
    grad_gains, grad_gate_up, grad_down, out_pieces, part_qkv = together(
        grad_gains, grad_gate_up, grad_down, out_pieces, part_qkv
    )
    if strided:
        grad_out = stacked([(piece, k, 0) for k, piece in enumerate(out_pieces)], w_out.shape)
    else:
        grad_out = out_pieces[0].astype(jnp.float32)
    grad_gains = butterfly(grad_gains, "ctx")
    grad_gains = lax.dynamic_slice_in_dim(grad_gains, lax.axis_index("fsdp") * shard, shard, 1)
    if strided:
        grad_w_qkv = pl.pallas_call(
            functools.partial(write_heads, fsdp_count),
            grid=(3,),
            in_specs=[pl.BlockSpec((ctx_count, shard, own_width), lambda step: (0, 0, step))],
            out_specs=pl.BlockSpec((1, shard, width), lambda step: (step, 0, 0)),
            out_shape=jax.ShapeDtypeStruct((3, shard, width), jnp.float32),
            cost_estimate=free,
        )(part_qkv)
        grad_w_qkv = jnp.transpose(grad_w_qkv, (1, 0, 2))
    else:
        part_qkv = jnp.transpose(part_qkv.reshape(ctx_count, shard, 3, own_width), (1, 2, 0, 3))
        grad_w_qkv = part_qkv.reshape(w_qkv.shape).astype(jnp.float32)
    return (
        layer_out[None],
        input_grad[None],
        grad_gains[0],
        grad_w_qkv,
        grad_out,
        grad_gains[1],
        grad_gate_up,
        grad_down,
    )


def solution(mesh):
    return jax.shard_map(
        per_device,
        mesh=mesh,
        in_specs=(
            P("fsdp", "ctx", None),
            P("fsdp", "ctx", None),
            P("fsdp", "ctx"),
            P("fsdp", None),
            P("fsdp"),
            P("fsdp", None, None),
            P("fsdp", None),
            P("fsdp"),
            P("fsdp", None, None),
            P("fsdp", None),
        ),
        out_specs=(
            P("fsdp", "ctx", None),
            P("fsdp", "ctx", None),
            P("fsdp"),
            P("fsdp", None, None),
            P("fsdp", None),
            P("fsdp"),
            P("fsdp", None, None),
            P("fsdp", None),
        ),
        check_vma=False,
    )
```

```python
import functools

import jax
import jax.numpy as jnp
from jax import lax
from jax.experimental import pallas as pl
from jax.experimental.pallas import tpu as pltpu
from jax.sharding import PartitionSpec as P

HD = 64

rope_theta = 130000.0
norm_eps = 1e-05
score_scale = 0.125
masked_score = -1e30
free = pl.CostEstimate(flops=1, bytes_accessed=1, transcendentals=0)


def swapped(array, axis, by):
    size = lax.axis_size(axis)
    return lax.ppermute(array, axis, [(i, i ^ by) for i in range(size)])


def gathered(array, axis):
    return [array] + [swapped(array, axis, k) for k in range(1, lax.axis_size(axis))]


def scattered(parts, axis):
    total = parts[0].astype(jnp.float32)
    for k in range(1, lax.axis_size(axis)):
        total = total + swapped(parts[k].astype(jnp.bfloat16), axis, k).astype(jnp.float32)
    return total


def paired(blocks):
    core = lax.axis_index("fsdp") % 2
    grid = blocks.reshape((blocks.shape[0] // 2, 2) + blocks.shape[1:])
    keep = lax.dynamic_index_in_dim(grid, core, 1, keepdims=False)
    got = swapped(lax.dynamic_index_in_dim(grid, 1 - core, 1, keepdims=False), "fsdp", 1)
    return jnp.stack([jnp.where(core == 0, keep, got), jnp.where(core == 0, got, keep)], 1)


def crossing(pairs):
    chip = lax.axis_index("fsdp") // 2
    return [
        lax.dynamic_index_in_dim(pairs, chip ^ k, 0, keepdims=False)
        for k in range(1, pairs.shape[0])
    ]


def crossed(sends, first=1):
    return [swapped(send, "fsdp", 2 * k) for k, send in enumerate(sends, first)]


def in_order(pairs, received):
    chip = lax.axis_index("fsdp") // 2
    for k, pair in enumerate(received, 1):
        pairs = lax.dynamic_update_index_in_dim(pairs, pair, chip ^ k, 0)
    return pairs.reshape((-1,) + pairs.shape[2:])


def first_hop(array):
    size = lax.axis_size("ctx")
    return [array] + [swapped(array, "ctx", k) for k in range(1, 3 if size == 4 else size)]


def second_hop(pieces):
    if lax.axis_size("ctx") != 4:
        return []
    half = pieces[0].shape[0] // 2
    return [swapped(pieces[1][:half], "ctx", 2), swapped(pieces[2][half:], "ctx", 1)]


def first_fold(parts):
    size = lax.axis_size("ctx")
    if size != 4:
        return [swapped(parts[k], "ctx", k) for k in range(1, size)]
    half = parts[0].shape[0] // 2
    return [swapped(parts[3][:half], "ctx", 1), swapped(parts[3][half:], "ctx", 2)]


def folded(parts, halves):
    if lax.axis_size("ctx") != 4:
        return []
    half = parts[0].shape[0] // 2
    over_x = jnp.concatenate([parts[1][:half], plus(parts[1][half:], halves[1])], 0)
    over_y = jnp.concatenate([plus(parts[2][:half], halves[0]), parts[2][half:]], 0)
    return [over_x, over_y]


def second_fold(sends, halves):
    if not sends:
        return halves
    return [swapped(sends[0], "ctx", 1), swapped(sends[1], "ctx", 2)]


def butterfly(array, axis):
    step = 1
    while step < lax.axis_size(axis):
        array = array + swapped(array, axis, step)
        step *= 2
    return array


def wide_fold(parts):
    size = lax.axis_size("ctx")
    if size != 4:
        return first_fold(parts)
    half = parts[0].shape[0] // 2
    return first_fold(parts) + [
        swapped(parts[1][:half], "ctx", 1),
        swapped(parts[2][half:], "ctx", 2),
    ]


def late_terms(parts, arrived):
    if lax.axis_size("ctx") != 4:
        return []
    half = parts[0].shape[0] // 2
    return [plus(parts[1][half:], arrived[1]), plus(parts[2][:half], arrived[0])]


def late_fold(terms):
    return [swapped(term, "ctx", k) for k, term in enumerate(terms, 1)]


def wide_sum(own, arrived, late):
    if not late:
        return plus(own, *arrived)
    half = own.shape[0] // 2
    return jnp.concatenate(
        [plus(own[:half], arrived[2], late[1]), plus(own[half:], arrived[3], late[0])], 0
    )


def paired_sum(terms):
    while len(terms) > 1:
        terms = [terms[i] + terms[i + 1] for i in range(0, len(terms), 2)]
    return terms[0]


def plus(*terms):
    return low(sum(term.astype(jnp.float32) for term in terms))


def placed(pieces, shape, block, body, result=None):
    own = jnp.stack([lax.axis_index("ctx"), lax.axis_index("fsdp") // 2]).astype(jnp.int32)
    for piece, k, index in pieces:

        def out_map(step, own_ref, k=k, index=index):
            return index(own_ref[0] ^ k, own_ref[1], step)

        in_specs = [pl.BlockSpec((1,) + piece.shape[1:], lambda step, own_ref: (step, 0, 0))]
        operands = [own, piece]
        aliases = {}
        if result is not None:
            in_specs.append(pl.BlockSpec(memory_space=pl.ANY))
            operands.append(result)
            aliases = {2: 0}
        result = pl.pallas_call(
            body,
            grid_spec=pltpu.PrefetchScalarGridSpec(
                num_scalar_prefetch=1,
                grid=(piece.shape[0],),
                in_specs=in_specs,
                out_specs=pl.BlockSpec(block, out_map),
            ),
            out_shape=jax.ShapeDtypeStruct(shape, jnp.float32),
            input_output_aliases=aliases,
            cost_estimate=free,
        )(*operands)
    return result


def write_pair(own_ref, piece_ref, *refs):
    out_ref = refs[-1]
    half = piece_ref.shape[2] // 2
    out_ref[:, 0, :] = piece_ref[0, :, :half].astype(jnp.float32)
    out_ref[:, 1, :] = piece_ref[0, :, half:].astype(jnp.float32)


def write_rows(own_ref, piece_ref, *refs):
    refs[-1][...] = piece_ref[0].astype(jnp.float32)


def stacked(pieces, shape):
    own = lax.axis_index("ctx").astype(jnp.int32)[None]
    each = shape[0] // lax.axis_size("ctx")

    def body(own_ref, *refs):
        for ref, (piece, k, row) in zip(refs, pieces):
            start = pl.multiple_of((own_ref[0] ^ k) * each + row, 16)
            refs[-1][pl.ds(start, piece.shape[0]), :] = ref[...].astype(jnp.float32)

    return pl.pallas_call(
        body,
        grid_spec=pltpu.PrefetchScalarGridSpec(
            num_scalar_prefetch=1,
            grid=(1,),
            in_specs=[
                pl.BlockSpec(piece.shape, lambda step, own_ref: (0, 0)) for piece, _, _ in pieces
            ],
            out_specs=pl.BlockSpec(shape, lambda step, own_ref: (0, 0)),
        ),
        out_shape=jax.ShapeDtypeStruct(shape, jnp.float32),
        cost_estimate=free,
    )(own, *[piece for piece, _, _ in pieces])


def angles(positions, width):
    half_width = width // 2
    frequency = rope_theta ** (-2.0 * jnp.arange(half_width, dtype=jnp.float32) / width)
    phases = positions.astype(jnp.float32)[:, None] * frequency[None, :]
    return (jnp.cos(phases)[:, None, :], jnp.sin(phases)[:, None, :])


def rotate(values, cosine, sine):
    half_width = values.shape[-1] // 2
    leading = values[..., :half_width]
    trailing = values[..., half_width:]
    return jnp.concatenate(
        [leading * cosine - trailing * sine, trailing * cosine + leading * sine], -1
    )


def inverse_rms(values):
    return lax.rsqrt(jnp.mean(values * values, -1, keepdims=True) + norm_eps)


def norm_back(grad_normed, normed, gain, inverse):
    scaled = grad_normed * gain
    return inverse * (scaled - normed * jnp.mean(scaled * normed, -1, keepdims=True))


def product(left, right, left_dim, right_dim):
    return lax.dot_general(
        left, right, (((left_dim,), (right_dim,)), ((), ())), preferred_element_type=jnp.float32
    )


def low(values):
    return values.astype(jnp.bfloat16)


def together(*arrays):
    return lax.optimization_barrier(arrays)


def gather_rows(array, axis):
    return lax.all_gather(array, axis, axis=0, tiled=True)


def scatter_rows(array, axis):
    return lax.psum_scatter(low(array), axis, scatter_dimension=0, tiled=True)


def write_heads(groups, piece_ref, out_ref):
    count = piece_ref.shape[0]
    each = piece_ref.shape[2] // groups
    for group in range(groups):
        row = [
            piece_ref[index, :, group * each : (group + 1) * each].astype(jnp.float32)
            for index in range(count)
        ]
        out_ref[0, :, group * count * each : (group + 1) * count * each] = jnp.concatenate(row, 1)


def own_columns(own_ref, in_ref, out_ref):
    half = in_ref.shape[2]
    out_ref[0, :, :half] = in_ref[:, 0, :]
    out_ref[0, :, half:] = in_ref[:, 1, :]


def per_device(
    tokens, cotangent, block_ids, span_order, attn_gain, w_qkv, w_out, ffn_gain, w_gate_up, w_down
):
    ctx_count = lax.axis_size("ctx")
    fsdp_count = lax.axis_size("fsdp")
    ctx = lax.axis_index("ctx")
    rows = tokens.shape[1]
    width = tokens.shape[2]
    shard = w_qkv.shape[0]
    length = rows * ctx_count
    heads = width // HD // ctx_count
    own_width = heads * HD
    strided = (shard // HD) % ctx_count == 0

    chunks = jnp.bitwise_xor(ctx, jnp.arange(ctx_count, dtype=jnp.int32))
    order_row = span_order[0]
    spans = order_row.shape[0]
    half = length // spans
    local = jnp.arange(rows, dtype=jnp.int32)
    slots = (chunks[:, None] * (rows // half) + (local // half)[None, :]).reshape(length)
    matches = slots[:, None] == jnp.arange(spans, dtype=jnp.int32)[None, :]
    picked = jnp.sum(jnp.where(matches, order_row[None, :], 0), axis=1)
    positions = picked * half + jnp.tile(local % half, ctx_count)
    cosine, sine = angles(positions, HD)
    if strided:
        per = heads // fsdp_count
        qkv_own = lax.dynamic_index_in_dim(
            w_qkv.reshape(shard, 3, fsdp_count, ctx_count, per * HD), ctx, 3, keepdims=False
        ).reshape(shard, 3 * own_width)
        out_own = lax.dynamic_slice_in_dim(w_out, ctx * (per * HD), per * HD, 0)
        qkv_weight = gather_rows(qkv_own, "fsdp")
        out_weight = gather_rows(out_own, "fsdp")
    else:
        qkv_own = lax.dynamic_slice_in_dim(w_qkv, ctx * own_width, own_width, 2)
        qkv_weight = gather_rows(qkv_own.reshape(shard, 3 * own_width), "fsdp")
        out_weight = lax.dynamic_slice_in_dim(
            gather_rows(w_out, "fsdp"), ctx * own_width, own_width, 0
        )
    hidden_own = w_down.shape[0]
    part = shard // ctx_count
    gate_up_own = pl.pallas_call(
        own_columns,
        grid_spec=pltpu.PrefetchScalarGridSpec(
            num_scalar_prefetch=1,
            grid=(fsdp_count,),
            in_specs=[pl.BlockSpec((part, 2, hidden_own), lambda step, own: (own[0], 0, step))],
            out_specs=pl.BlockSpec((1, part, 2 * hidden_own), lambda step, own: (step, 0, 0)),
        ),
        out_shape=jax.ShapeDtypeStruct((fsdp_count, part, 2 * hidden_own), jnp.bfloat16),
        cost_estimate=free,
    )(ctx.astype(jnp.int32)[None], w_gate_up)
    gate_up_own = paired(gate_up_own)
    gate_up_sends = crossing(gate_up_own)
    gate_up_sends, gains, own_tokens = together(
        gate_up_sends, jnp.stack([attn_gain, ffn_gain]), tokens[0]
    )
    gate_up_mine = in_order(gate_up_own, crossed(gate_up_sends))
    gate_up_mine = gate_up_mine.reshape(fsdp_count * part, 2 * hidden_own)
    seq_inputs = jnp.concatenate(gathered(own_tokens, "ctx"), 0)
    gains = lax.all_gather(gains, "fsdp", axis=1, tiled=True).astype(jnp.float32)
    gain_one, gain_two = gains[0], gains[1]
    own_blocks, seq_inputs = together(block_ids[0], seq_inputs)
    blocks = jnp.concatenate(gathered(own_blocks, "ctx"), 0)
    allowed = (blocks[None, :] <= blocks[:, None])[None]
    gate_up_mine, qkv_weight = together(gate_up_mine, qkv_weight)
    gate_up_pieces = first_hop(gate_up_mine)

    def to_parts(array):
        lead = array.shape[:-1]
        array = array.reshape(lead + (fsdp_count, ctx_count, part))
        array = jnp.swapaxes(array, -3, -2).reshape(lead + (ctx_count, fsdp_count * part))
        return jnp.concatenate(
            [
                lax.dynamic_index_in_dim(array, ctx ^ k, array.ndim - 2, keepdims=False)
                for k in range(ctx_count)
            ],
            -1,
        )

    def from_parts(array):
        lead = array.shape[:-1]
        array = array.reshape(lead + (ctx_count, fsdp_count * part))
        array = jnp.stack(
            [
                lax.dynamic_index_in_dim(array, ctx ^ k, array.ndim - 2, keepdims=False)
                for k in range(ctx_count)
            ],
            -2,
        )
        array = array.reshape(lead + (ctx_count, fsdp_count, part))
        return jnp.swapaxes(array, -3, -2).reshape(lead + (width,))

    seq_inputs = seq_inputs.astype(jnp.float32)
    seq_inverse = inverse_rms(seq_inputs)
    seq_normed = seq_inputs * seq_inverse
    act_seq = low(seq_normed * gain_one)
    inputs, inverse_one, normed_one = seq_inputs[:rows], seq_inverse[:rows], seq_normed[:rows]
    qkv = product(act_seq, qkv_weight, 1, 0).reshape(length, 3, heads, HD)
    query = low(rotate(qkv[:, 0], cosine, sine))
    keys = low(rotate(qkv[:, 1], cosine, sine))
    values = low(qkv[:, 2])
    scores = (
        jnp.einsum("qhe,khe->hqk", query, keys, preferred_element_type=jnp.float32) * score_scale
    )
    scores = jnp.where(allowed, scores, masked_score)
    top = jnp.max(scores, -1, keepdims=True)
    weights = jnp.where(allowed, jnp.exp(scores - top), 0.0)
    total = jnp.sum(weights, -1, keepdims=True)
    probs = weights / total
    probs_b = low(probs)
    attended = jnp.einsum("hqk,khe->qhe", probs_b, values, preferred_element_type=jnp.float32)
    attn_b = low(attended).reshape(length, own_width)
    branch = product(attn_b, out_weight, 1, 0).reshape(ctx_count, rows, width)
    resid = inputs + scattered([branch[k] for k in range(ctx_count)], "ctx")

    inverse_two = inverse_rms(resid)
    normed_two = resid * inverse_two
    act_two = to_parts(low(normed_two * gain_two))
    cot = gather_rows(cotangent[0], "fsdp")
    act_two, cot, gate_up_pieces = together(act_two, cot, gate_up_pieces)
    act_two = gather_rows(act_two, "fsdp")
    gate_up_weight = jnp.concatenate(gate_up_pieces + second_hop(gate_up_pieces), 0)
    gate_up = product(act_two, gate_up_weight, 1, 0)
    gate = gate_up[:, :hidden_own]
    upward = gate_up[:, hidden_own:]
    sigma = jax.nn.sigmoid(gate)
    swish = gate * sigma
    hidden = low(swish * upward)
    block = hidden_own // ctx_count
    grad_hidden = product(cot, w_down, 1, 1)
    grad_gate = grad_hidden * upward * sigma * (1.0 + gate * (1.0 - sigma))
    grad_up = grad_hidden * swish
    grad_gu = low(jnp.concatenate([grad_gate, grad_up], 1))
    span = fsdp_count * part

    def gu_term(k):
        return low(product(act_two[:, k * span : (k + 1) * span], grad_gu, 0, 0))

    grad_act_two = low(product(grad_gu, gate_up_weight, 1, 1))
    gu_final = gu_term(ctx_count - 1)
    grad_act_two, grad_gu, gu_final = together(grad_act_two, grad_gu, gu_final)
    grad_act_two = scatter_rows(grad_act_two, "fsdp")
    part_gu = [gu_term(k) for k in range(ctx_count - 1)] + [gu_final]
    gu_arrived = wide_fold(part_gu)
    out_part = low(product(hidden, w_down, 1, 0))
    part_down = low(product(hidden, cot, 0, 0)).reshape(ctx_count, block, width)
    part_down = [
        lax.dynamic_index_in_dim(part_down, ctx ^ k, 0, keepdims=False) for k in range(ctx_count)
    ]
    part_gu, gu_arrived, out_part, part_down = together(part_gu, gu_arrived, out_part, part_down)
    gu_terms = late_terms(part_gu, gu_arrived)
    grad_act_two, out_part = together(grad_act_two, out_part)
    gu_late = late_fold(gu_terms)
    layer_part = scatter_rows(out_part, "fsdp")
    grad_act_two = from_parts(grad_act_two).astype(jnp.float32)
    grad_gain_two = jnp.sum(grad_act_two * normed_two, 0)
    grad_resid = cotangent[0].astype(jnp.float32) + norm_back(
        grad_act_two, normed_two, gain_two, inverse_two
    )

    grad_branch = jnp.concatenate(gathered(low(grad_resid), "ctx"), 0)
    grad_branch, gu_late, part_down = together(grad_branch, gu_late, part_down)
    down_halves = first_fold(part_down)
    gu_sum = wide_sum(part_gu[0], gu_arrived, gu_late)
    gu_pairs = paired(gu_sum.reshape(fsdp_count, part, 2 * hidden_own))
    part_out = low(product(attn_b, grad_branch, 0, 0))
    grad_att = low(product(grad_branch, out_weight, 1, 1)).reshape(length, heads, HD)
    gu_sends = crossing(gu_pairs)
    grad_att, part_out, gu_pairs, gu_sends, down_halves = together(
        grad_att, part_out, gu_pairs, gu_sends, down_halves
    )
    gu_received = crossed(gu_sends)
    down_last = second_fold(folded(part_down, down_halves), down_halves)
    part_out = scatter_rows(part_out, "fsdp") if strided else part_out
    delta = jnp.sum(grad_att.astype(jnp.float32) * attended, -1)
    grad_probs = jnp.einsum("qhe,khe->hqk", grad_att, values, preferred_element_type=jnp.float32)
    grad_scores = low(probs * (grad_probs - delta.T[..., None]))
    grad_scores, gu_received[:1] = together(grad_scores, gu_received[:1])
    gu_own = lax.dynamic_index_in_dim(gu_pairs, lax.axis_index("fsdp") // 2, 0, keepdims=False)
    chips = len(gu_received) + 1
    gu_near = first_hop(jnp.concatenate([gu_own] + gu_received[: chips // 2 - 1], 0))
    grad_values = jnp.einsum("hqk,qhe->khe", probs_b, grad_att, preferred_element_type=jnp.float32)
    grad_query = (
        jnp.einsum("hqk,khe->qhe", grad_scores, keys, preferred_element_type=jnp.float32)
        * score_scale
    )
    grad_keys = (
        jnp.einsum("hqk,qhe->khe", grad_scores, query, preferred_element_type=jnp.float32)
        * score_scale
    )
    grad_qkv = low(
        jnp.stack(
            [rotate(grad_query, cosine, -sine), rotate(grad_keys, cosine, -sine), grad_values], 1
        )
    ).reshape(length, 3 * own_width)
    part_qkv = low(product(act_seq, grad_qkv, 0, 0))
    back = low(product(grad_qkv, qkv_weight, 1, 1))
    grad_gain_one = jnp.sum(back.astype(jnp.float32) * seq_normed, 0)
    grad_gains = jnp.stack([grad_gain_one, grad_gain_two])
    back = back.reshape(ctx_count, rows, width)
    back = [back[k] for k in range(ctx_count)]
    part_qkv, back, grad_gains, down_last, layer_part, gu_received[::2], gu_near = together(
        part_qkv, back, grad_gains, down_last, layer_part, gu_received[::2], gu_near
    )

    back_halves = first_fold(back)
    down_pieces = first_hop(plus(part_down[0], *down_last))
    part_qkv, part_out, back_halves, gu_received, down_pieces = together(
        part_qkv, part_out, back_halves, gu_received, down_pieces
    )
    part_qkv = scatter_rows(part_qkv, "fsdp")
    gu_far = first_hop(jnp.concatenate(gu_received[chips // 2 - 1 :], 0))
    back_last = second_fold(folded(back, back_halves), back_halves)
    grad_act_one = sum(term.astype(jnp.float32) for term in [back[0]] + back_last)
    if ctx_count == 4:
        gu_near.append(swapped(gu_near[1], "ctx", 2))
    grad_act_one, gu_near[:3] = together(grad_act_one, gu_near[:3])
    layer_out = low(resid + layer_part.astype(jnp.float32))
    input_grad = low(grad_resid + norm_back(grad_act_one, normed_one, gain_one, inverse_one))

    def gate_up_columns(offset):
        return lambda other, chip, step: (other, 0, 2 * (chip ^ (offset + step // 2)) + step % 2)

    grad_gate_up = placed(
        [(piece, k, gate_up_columns(0)) for k, piece in enumerate(gu_near[:3])],
        w_gate_up.shape,
        (part, 2, hidden_own),
        write_pair,
    )
    gu_far, gu_near, layer_out, input_grad, down_pieces, grad_gate_up, part_qkv = together(
        gu_far, gu_near, layer_out, input_grad, down_pieces, grad_gate_up, part_qkv
    )
    part_qkv = lax.all_gather(part_qkv, "ctx", axis=0)
    if ctx_count == 4:
        gu_far.append(swapped(gu_far[2], "ctx", 1))
    down_last = second_hop(down_pieces)
    grad_gate_up = placed(
        [(piece, k, gate_up_columns(0)) for k, piece in enumerate(gu_near) if k > 2]
        + [(piece, k, gate_up_columns(chips // 2)) for k, piece in enumerate(gu_far[:3])],
        w_gate_up.shape,
        (part, 2, hidden_own),
        write_pair,
        grad_gate_up,
    )
    rows_each = block // 2

    def down_rows(offset):
        return lambda other, chip, step: (other * 2 + offset + step, 0)

    grad_down = placed(
        [
            (piece.reshape(2, rows_each, width), k, down_rows(0))
            for k, piece in enumerate(down_pieces)
        ],
        w_down.shape,
        (rows_each, width),
        write_rows,
    )
    grad_gate_up, grad_down, grad_gains = together(grad_gate_up, grad_down, grad_gains)
    grad_gains = butterfly(grad_gains, "fsdp")
    gu_far, down_last, grad_gate_up, grad_down, grad_gains = together(
        gu_far, down_last, grad_gate_up, grad_down, grad_gains
    )
    if strided:
        out_pieces = gathered(part_out, "ctx")
    else:
        out_pieces = [scatter_rows(gather_rows(part_out, "ctx"), "fsdp")]
    grad_gate_up = placed(
        [(piece, k, gate_up_columns(chips // 2)) for k, piece in enumerate(gu_far) if k > 2],
        w_gate_up.shape,
        (part, 2, hidden_own),
        write_pair,
        grad_gate_up,
    )
    grad_down = placed(
        [(piece[None], 3, down_rows(k)) for k, piece in enumerate(down_last)],
        w_down.shape,
        (rows_each, width),
        write_rows,
        grad_down,
    )
    grad_gains, grad_gate_up, grad_down, out_pieces, part_qkv = together(
        grad_gains, grad_gate_up, grad_down, out_pieces, part_qkv
    )
    if strided:
        grad_out = stacked([(piece, k, 0) for k, piece in enumerate(out_pieces)], w_out.shape)
    else:
        grad_out = out_pieces[0].astype(jnp.float32)
    grad_gains = paired_sum(gathered(grad_gains, "ctx"))
    grad_gains = lax.dynamic_slice_in_dim(grad_gains, lax.axis_index("fsdp") * shard, shard, 1)
    if strided:
        grad_w_qkv = pl.pallas_call(
            functools.partial(write_heads, fsdp_count),
            grid=(3,),
            in_specs=[pl.BlockSpec((ctx_count, shard, own_width), lambda step: (0, 0, step))],
            out_specs=pl.BlockSpec((1, shard, width), lambda step: (step, 0, 0)),
            out_shape=jax.ShapeDtypeStruct((3, shard, width), jnp.float32),
            cost_estimate=free,
        )(part_qkv)
        grad_w_qkv = jnp.transpose(grad_w_qkv, (1, 0, 2))
    else:
        part_qkv = jnp.transpose(part_qkv.reshape(ctx_count, shard, 3, own_width), (1, 2, 0, 3))
        grad_w_qkv = part_qkv.reshape(w_qkv.shape).astype(jnp.float32)
    return (
        layer_out[None],
        input_grad[None],
        grad_gains[0],
        grad_w_qkv,
        grad_out,
        grad_gains[1],
        grad_gate_up,
        grad_down,
    )


def solution(mesh):
    return jax.shard_map(
        per_device,
        mesh=mesh,
        in_specs=(
            P("fsdp", "ctx", None),
            P("fsdp", "ctx", None),
            P("fsdp", "ctx"),
            P("fsdp", None),
            P("fsdp"),
            P("fsdp", None, None),
            P("fsdp", None),
            P("fsdp"),
            P("fsdp", None, None),
            P("fsdp", None),
        ),
        out_specs=(
            P("fsdp", "ctx", None),
            P("fsdp", "ctx", None),
            P("fsdp"),
            P("fsdp", None, None),
            P("fsdp", None),
            P("fsdp"),
            P("fsdp", None, None),
            P("fsdp", None),
        ),
        check_vma=False,
    )
```
